32 devices in a mesh: wide: 4 (over y, x), grp: 8 (over z, core).
Axes of the slice: x: 2, y: 2, z: 4, core: 2. Of those that a mesh axis runs over, the one named last changes fastest.
Arguments:
- shapes: float32 [64, 3, 312], P(('wide', 'grp')), may hold values from -10 to 10
- density: float32 [64, 3, 312], P(('wide', 'grp')), may hold values from -6 to 6
- quad_weight: float32 [64, 312], P(('wide', 'grp')), may hold values from 0.013 to 0.13
- live: int32 [64], P(('wide', 'grp')), may hold values from 0 to 1, as said below
- neighbor: int32 [64, 64], P(('wide', 'grp')), may hold values from 0 to 1
- rotation: bfloat16 [312, 312], replicated, may hold values from 0 to 1
Outputs:
- self_ops: bfloat16 [64, 3, 312, 3, 312], P(('wide', 'grp'))
- velocity: float32 [64, 3, 312], P(('wide', 'grp'))
The draws below stay inside these ranges and needn't reach their ends.
Inputs may be any that keep to these rules, and one draw needn't show every extreme that they name: Exactly 8 of the 16 slots held by the devices of one index of wide are live.
All inputs are finite; a program needn't handle non-finite values.
Results may differ from the reference program's by a relative error of at most 0.0036.
Values may be sent and summed in bfloat16 or wider, within the bound.
A program may use at most 64 MiB of HBM per device.

```python
import math
import jax
import jax.numpy as jnp
from jax import lax

POINTS = 312
CAPS = 64
GROUP_SLOTS = 16
LIVE_SLOTS = 8


def draw_shapes(key, part):
    key_center, key_cloud = jax.random.split(jax.random.fold_in(key, 11))
    centers = jax.random.uniform(key_center, (CAPS, 3, 1), jnp.float32, -6.0, 6.0)
    cloud = jnp.clip(2.5 * jax.random.normal(key_cloud, (CAPS, 3, POINTS), jnp.float32), -4.0, 4.0)
    return centers + cloud


def draw_rotation(key, part):
    raw_table = jax.random.uniform(jax.random.fold_in(key, 12), (POINTS, POINTS), jnp.float32, 0.2, 1.0)
    spread = raw_table / jnp.sum(raw_table, axis=1, keepdims=True)
    return (0.5 * jnp.eye(POINTS, dtype=jnp.float32) + 0.5 * spread).astype(jnp.bfloat16)


def draw_live(key, part):
    group_keys = jax.random.split(jax.random.fold_in(key, 13), CAPS // GROUP_SLOTS)
    orders = jax.vmap(lambda single: jax.random.permutation(single, GROUP_SLOTS))(group_keys)
    return (orders < LIVE_SLOTS).astype(jnp.int32).reshape(CAPS)


def draw_neighbor(key, part):
    key_level, key_pairs = jax.random.split(jax.random.fold_in(key, 14))
    level = jax.random.randint(key_level, (CAPS, 1), 1, 6)
    raw_pairs = jax.random.randint(key_pairs, (CAPS, CAPS), 0, 8)
    return (raw_pairs < level).astype(jnp.int32)


def levels(key, shape, cuts, least, high):
    def one(dim, blocks):
        steps = jax.random.uniform(jax.random.fold_in(jax.random.fold_in(key, 6), dim), (blocks,), jnp.float32, least / len(cuts), high / len(cuts))
        return jnp.repeat(jnp.exp(steps), shape[dim] // blocks).reshape((-1,) + (1,) * (len(shape) - dim - 1))

    loudness = one(*cuts[0])
    for cut in cuts[1:]:
        loudness = loudness * one(*cut)
    return loudness


def centred(rng, shape, scale, bound, cuts=(), kind=jnp.bfloat16):
    level = levels(rng, shape, cuts, -0.22, 0.18) if cuts else 1.0
    values = jax.random.normal(rng, shape, jnp.float32) * scale * level
    return jnp.minimum(jnp.maximum(values, -bound), bound).astype(kind)


def setup_inputs(seed: int = 0) -> dict:
    keys = jax.random.split(jax.random.key(seed), 7)
    shapes = draw_shapes(jax.random.fold_in(keys[6], 71), 0)
    density = centred(keys[1], (CAPS, 3, POINTS), 1.0, 6.0, ((0, 32),), jnp.float32)
    quad_weight = jnp.clip(jnp.exp(math.log(0.13) - 2.30258504 * jax.random.uniform(keys[2], (CAPS, POINTS), jnp.float32) ** levels(keys[2], (CAPS, POINTS), ((0, 32),), -0.2, 0.2)), 0.013, 0.13)
    live = draw_live(jax.random.fold_in(keys[6], 71), 0)
    neighbor = draw_neighbor(jax.random.fold_in(keys[6], 71), 0)
    rotation = draw_rotation(jax.random.fold_in(keys[6], 71), 0)
    return {"shapes": shapes, "density": density, "quad_weight": quad_weight, "live": live, "neighbor": neighbor, "rotation": rotation}


soft_square = 0.0625

def kernel_block(targets, quad_nodes, weights):
    offset = targets[:, :, :, None] - quad_nodes[:, :, None, :]
    dist_sq = lax.optimization_barrier(jnp.sum(offset * offset, axis=1))
    inv_cube = lax.rsqrt(dist_sq + soft_square) ** 3
    scaled = inv_cube * weights[:, None, :]
    outer_prod = offset[:, :, None] * offset[:, None, :]
    unit_eye = jnp.eye(3, dtype=jnp.float32)
    kernel_full = (unit_eye[None, :, :, None, None] * (dist_sq + 2.0 * soft_square)[:, None, None] + outer_prod) * scaled[:, None, None]
    return kernel_full.transpose(0, 1, 3, 2, 4)

def build_ops(targets, shapes, weights, rotation):
    rot_wide = rotation.astype(jnp.float32)
    quad_nodes = jnp.einsum('cak,jk->caj', shapes, rot_wide, precision=lax.Precision.HIGHEST)
    kernel = kernel_block(targets, quad_nodes, weights).astype(jnp.bfloat16)
    leading = kernel.shape[:4]
    flattened = kernel.reshape(-1, kernel.shape[4])
    product = jnp.dot(flattened, rotation, preferred_element_type=jnp.float32)
    return product.reshape(leading + (rotation.shape[1],)).astype(jnp.bfloat16)

def pair_velocity(targets, src_position, src_strength):
    offset = targets[:, :, None] - src_position[:, None, :]
    dist_sq = lax.optimization_barrier(jnp.sum(offset * offset, axis=0))
    inv_cube = lax.rsqrt(dist_sq + soft_square) ** 3
    projected = lax.optimization_barrier(jnp.sum(offset * src_strength[:, None, :], axis=0))
    pair_terms = (src_strength[:, None, :] * (dist_sq + 2.0 * soft_square)[None] + offset * projected[None]) * inv_cube[None]
    return lax.optimization_barrier(jnp.sum(pair_terms, axis=2))

def reference(shapes, density, quad_weight, live, neighbor, rotation):
    capsule_count = shapes.shape[0]
    points = shapes.shape[2]
    live_f = live.astype(jnp.float32)
    dens_half = lax.optimization_barrier(density.astype(jnp.bfloat16)).astype(jnp.float32)

    def one_capsule(element):
        shape_one, weight_one, live_flag, dens_one = element
        built = build_ops(shape_one[None], shape_one[None], weight_one[None], rotation)[0]
        built = jnp.where(live_flag > 0, built, jnp.zeros_like(built))
        self_part = jnp.einsum('aibj,bj->ai', built.astype(jnp.float32), dens_one)
        return (built, self_part)
    self_ops, self_velocity = lax.map(one_capsule, (shapes, quad_weight, live, dens_half))
    strength = quad_weight[:, None, :] * density * live_f[:, None, None]
    flat_targets = shapes.transpose(1, 0, 2).reshape(3, capsule_count * points)
    target_ids = jnp.arange(capsule_count, dtype=jnp.int32)
    mask_f = neighbor.astype(jnp.float32)

    def add_source(running, element):
        src_position, src_strength, column, source = element
        velocity_part = pair_velocity(flat_targets, src_position, src_strength).reshape(3, capsule_count, points)
        factor = jnp.where(target_ids == source, jnp.zeros_like(column), column)
        return (running + velocity_part * factor[None, :, None], None)
    start = jnp.zeros((3, capsule_count, points), jnp.float32)
    mutual, unused_out = lax.scan(add_source, start, (shapes, strength, mask_f.T, target_ids))
    velocity = (self_velocity + mutual.transpose(1, 0, 2)) * live_f[:, None, None]
    return (self_ops, velocity)
```

```python
import functools
import jax
import jax.numpy as jnp
from jax import lax
from jax.experimental import pallas as pl
from jax.experimental.pallas import tpu as pltpu
from jax.sharding import PartitionSpec as P

soft_square = 0.0625
MESH = pl.DeviceIdType.MESH
SYM = ((0, 0), (0, 1), (0, 2), (1, 1), (1, 2), (2, 2))


def up(value, step):
    return (value + step - 1) // step * step


def split3(x):
    hi = x.astype(jnp.bfloat16)
    rest = x - hi.astype(jnp.float32)
    mid = rest.astype(jnp.bfloat16)
    low = (rest - mid.astype(jnp.float32)).astype(jnp.bfloat16)
    return hi, mid, low


def gather_kernel(
    slots, grp, wide, rows,
    pk_ref, qw_ref, dens_ref, rot_ref,
    ops_ref, vel_ref, tgt_ref, src_ref, mask_ref,
    gbuf, wbuf, kern, cols, gsend, grecv, wsend, wrecv,
):
    n = rot_ref.shape[0]
    me_g = lax.axis_index("grp")
    me_w = lax.axis_index("wide")
    barrier = pltpu.get_barrier_semaphore()
    for off in range(1, grp):
        pl.semaphore_signal(
            barrier, inc=1, device_id={"grp": lax.rem(me_g + off, grp)}, device_id_type=MESH
        )
    for off in range(1, wide):
        pl.semaphore_signal(
            barrier, inc=1, device_id={"wide": lax.rem(me_w + off, wide)}, device_id_type=MESH
        )
    pl.semaphore_wait(barrier, grp + wide - 2)
    copies = []
    for off in range(1, grp):
        copies.append(
            pltpu.make_async_remote_copy(
                src_ref=pk_ref.at[pl.ds(0, rows)],
                dst_ref=gbuf.at[me_g],
                send_sem=gsend.at[off],
                recv_sem=grecv.at[off],
                device_id={"grp": lax.rem(me_g + off, grp)},
                device_id_type=MESH,
            )
        )
    for off in range(1, wide):
        copies.append(
            pltpu.make_async_remote_copy(
                src_ref=pk_ref,
                dst_ref=wbuf.at[me_w],
                send_sem=wsend.at[off],
                recv_sem=wrecv.at[off],
                device_id={"wide": lax.rem(me_w + off, wide)},
                device_id_type=MESH,
            )
        )
    for copy in copies:
        copy.start()

    rot = rot_ref[...]
    for c in range(slots):
        place = jnp.concatenate([pk_ref[a * slots + c : a * slots + c + 1, :] for a in range(3)], axis=0)
        pos = place[:, :n]
        nodes = None
        for piece in split3(pos):
            part = lax.dot_general(
                piece, rot, (((1,), (1,)), ((), ())), preferred_element_type=jnp.float32
            )
            nodes = part if nodes is None else nodes + part
        weight = qw_ref[c : c + 1, :]
        tall = jnp.concatenate([place, jnp.zeros((5, place.shape[1]), jnp.float32)], axis=0)
        cols[...] = jnp.transpose(tall)

        def chunk(step, carry):
            start = pl.multiple_of(step * 16, 16)
            block = cols[pl.ds(start, 16), :]
            diff = [block[:, a : a + 1] - nodes[a : a + 1, :] for a in range(3)]
            dist = diff[0] * diff[0] + diff[1] * diff[1] + diff[2] * diff[2]
            inv = lax.rsqrt(dist + soft_square)
            scaled = inv * inv * inv * weight
            half = [d * scaled for d in diff]
            diag = (dist + 2.0 * soft_square) * scaled
            for index, (a, b) in enumerate(SYM):
                value = half[a] * diff[b]
                if a == b:
                    value = value + diag
                kern[index, pl.ds(start, 16), :] = value.astype(jnp.bfloat16)
            return carry

        lax.fori_loop(0, kern.shape[1] // 16, chunk, 0)
        alive = pk_ref[rows + 3 * slots + c : rows + 3 * slots + c + 1, :n]
        dens = jnp.concatenate(
            [dens_ref[b * slots + c : b * slots + c + 1, :] for b in range(3)], axis=0
        )
        dens = jnp.concatenate([dens, jnp.zeros((5, n), jnp.float32)], axis=0).astype(jnp.bfloat16)
        total = [None] * 3
        for index, (a, b) in enumerate(SYM):
            product = jnp.dot(kern[index], rot, preferred_element_type=jnp.float32)
            made = jnp.where(alive > 0.0, product, 0.0).astype(jnp.bfloat16)[:n]
            ops_ref[c, index] = made
            part = lax.dot_general(
                dens, made, (((1,), (1,)), ((), ())), preferred_element_type=jnp.float32
            )
            pieces = [(a, part[b : b + 1])]
            if a != b:
                pieces.append((b, part[a : a + 1]))
            for k, piece in pieces:
                total[k] = piece if total[k] is None else total[k] + piece
        for a in range(3):
            vel_ref[a * slots + c : a * slots + c + 1, :] = total[a]

    gbuf[me_g] = pk_ref[0:rows]
    wbuf[me_w] = pk_ref[...]
    for copy in copies:
        copy.wait()
    tgt_ref[...] = gbuf[...]
    src_ref[...] = wbuf[...]
    width = mask_ref.shape[1]
    for g in range(grp):
        for c in range(slots):
            mask_ref[g * slots + c : g * slots + c + 1, :] = gbuf[
                g, 3 * slots + c : 3 * slots + c + 1, 0:width
            ].astype(jnp.int32)
    for w in range(wide):
        for c in range(slots):
            row = grp * slots + w * slots + c
            mask_ref[row : row + 1, :] = wbuf[
                w, rows + 3 * slots + c : rows + 3 * slots + c + 1, 0:width
            ].astype(jnp.int32)


def pair_kernel(
    slots, grp, wide, rows,
    mask_ref, ops_ref, tgt_ref, src_ref,
    out_ref, acc_ref, spread, flip, aim, heap, order, sems,
):
    n = ops_ref.shape[2]
    lanes = tgt_ref.shape[2]
    me_g = lax.axis_index("grp")
    me_w = lax.axis_index("wide")
    copies = []
    for c in range(slots):
        for a in range(3):
            for b in range(3):
                index = SYM.index((min(a, b), max(a, b)))
                copies.append(
                    pltpu.make_async_copy(
                        ops_ref.at[c, index], out_ref.at[c, a, b], sems.at[len(copies)]
                    )
                )
    for copy in copies:
        copy.start()
    acc_ref[...] = jnp.zeros_like(acc_ref)
    heap[...] = jnp.zeros_like(heap)
    group = grp * slots
    for t in range(group):
        for a in range(3):
            row = a * slots + t % slots
            aim[t, a] = jnp.broadcast_to(tgt_ref[t // slots, row : row + 1, :], (8, lanes))
    panel = wide * slots

    for w in range(wide):
        flip[...] = jnp.transpose(src_ref[w])
        for c in range(slots):

            @pl.when(mask_ref[group + w * slots + c, 0] > 0)
            def _():
                for k in range(6):
                    row = k * slots + c if k < 3 else rows + (k - 3) * slots + c
                    spread[w * slots + c, k] = jnp.broadcast_to(
                        flip[0:n, row : row + 1], (n, 128)
                    )

    def scan_target(t, count):
        for s in range(panel):
            column = (s // slots * grp + me_g) * slots + s % slots
            hit = (
                (mask_ref[t, column] > 0)
                & (mask_ref[group + s, 0] > 0)
                & (me_w * group + t != column)
            )
            order[count] = t * panel + s
            count = count + hit.astype(jnp.int32)
        return count

    count = lax.fori_loop(0, group, scan_target, jnp.int32(0))
    tiles = lanes // 128

    def one_pair(p, carry):
        code = order[p]
        t, s = code // panel, code % panel
        xs = [
            [aim[t, a, :, l * 128 : l * 128 + 128] for a in range(3)] for l in range(tiles)
        ]

        def step(j, sums):
            start = pl.multiple_of(j * 8, 8)
            y = [spread[s, a, pl.ds(start, 8), :] for a in range(3)]
            f = [spread[s, 3 + a, pl.ds(start, 8), :] for a in range(3)]
            fresh = []
            for l in range(tiles):
                d = [xs[l][a] - y[a] for a in range(3)]
                dist = (d[0] * d[0] + d[1] * d[1]) + d[2] * d[2] + soft_square
                inv = lax.rsqrt(dist)
                cube = inv * inv * inv
                dot = d[0] * f[0] + d[1] * f[1] + d[2] * f[2]
                near = (dist + soft_square) * cube
                far = dot * cube
                for a in range(3):
                    fresh.append(sums[l * 3 + a] + (f[a] * near + d[a] * far))
            return tuple(fresh)

        zero = tuple(jnp.zeros((8, 128), jnp.float32) for _ in range(3 * tiles))
        steps = n // 8
        sums = lax.fori_loop(0, steps, step, zero, unroll=3 if steps % 3 == 0 else 1)
        for l in range(tiles):
            for a in range(3):
                here = (t, a, slice(0, 8), slice(l * 128, l * 128 + 128))
                heap[here] = heap[here] + sums[l * 3 + a]
        return carry

    lax.fori_loop(0, count, one_pair, 0)
    for t in range(group):
        for a in range(3):
            row = a * slots + t % slots
            acc_ref[t // slots, row : row + 1, :] = jnp.sum(heap[t, a], axis=0, keepdims=True)
    for copy in copies:
        copy.wait()


def scatter_kernel(slots, grp, part_ref, self_ref, live_ref, vel_ref, got, send, recv):
    n = self_ref.shape[1]
    me = lax.axis_index("grp")
    barrier = pltpu.get_barrier_semaphore()
    for off in range(1, grp):
        pl.semaphore_signal(
            barrier, inc=1, device_id={"grp": lax.rem(me + off, grp)}, device_id_type=MESH
        )
    pl.semaphore_wait(barrier, grp - 1)
    copies = []
    for off in range(1, grp):
        peer = lax.rem(me + off, grp)
        copies.append(
            pltpu.make_async_remote_copy(
                src_ref=part_ref.at[peer],
                dst_ref=got.at[off],
                send_sem=send.at[off],
                recv_sem=recv.at[off],
                device_id={"grp": peer},
                device_id_type=MESH,
            )
        )
    for copy in copies:
        copy.start()
    total = part_ref[me]
    for index, copy in enumerate(copies):
        copy.wait()
        total = total + got[index + 1]
    vel = self_ref[...] + total[0 : 3 * slots, :n]
    for a in range(3):
        for c in range(slots):
            row = a * slots + c
            alive = live_ref[3 * slots + c : 3 * slots + c + 1, :n]
            vel_ref[row : row + 1, :] = vel[row : row + 1] * alive


def on_device(shapes, density, quad_weight, live, neighbor, rotation):
    slots, _, n = shapes.shape
    caps = neighbor.shape[1]
    grp = lax.axis_size("grp")
    wide = lax.axis_size("wide")
    rows = up(4 * slots, 8)
    lanes = up(max(n, caps), 128)
    width = up(caps, 128)
    tall = up(n, 16)
    live_f = live.astype(jnp.float32)
    strength = quad_weight[:, None, :] * density * live_f[:, None, None]

    def rows_of(value):
        value = value.transpose(1, 0, 2).reshape(3 * slots, n)
        return jnp.pad(value, ((0, 0), (0, lanes - n)))

    fill = jnp.zeros((rows - 4 * slots, lanes), jnp.float32)
    mask = jnp.pad(neighbor.astype(jnp.float32) * live_f[:, None], ((0, 0), (0, lanes - caps)))
    packed = jnp.concatenate(
        [
            rows_of(shapes), mask, fill,
            rows_of(strength), jnp.broadcast_to(live_f[:, None], (slots, lanes)), fill,
        ],
        axis=0,
    )
    flat_density = density.transpose(1, 0, 2).reshape(3 * slots, n)
    vmem = pl.BlockSpec(memory_space=pltpu.VMEM)
    any_space = pl.BlockSpec(memory_space=pl.ANY)
    ops6, self_velocity, targets, sources, flags = pl.pallas_call(
        functools.partial(gather_kernel, slots, grp, wide, rows),
        out_shape=(
            jax.ShapeDtypeStruct((slots, 6, n, n), jnp.bfloat16),
            jax.ShapeDtypeStruct((3 * slots, n), jnp.float32),
            jax.ShapeDtypeStruct((grp, rows, lanes), jnp.float32),
            jax.ShapeDtypeStruct((wide, 2 * rows, lanes), jnp.float32),
            jax.ShapeDtypeStruct(((grp + wide) * slots, width), jnp.int32),
        ),
        in_specs=[vmem] * 4,
        out_specs=(vmem,) * 5,
        scratch_shapes=[
            pltpu.VMEM((grp, rows, lanes), jnp.float32),
            pltpu.VMEM((wide, 2 * rows, lanes), jnp.float32),
            pltpu.VMEM((6, tall, n), jnp.bfloat16),
            pltpu.VMEM((lanes, 8), jnp.float32),
            pltpu.SemaphoreType.DMA((grp,)),
            pltpu.SemaphoreType.DMA((grp,)),
            pltpu.SemaphoreType.DMA((wide,)),
            pltpu.SemaphoreType.DMA((wide,)),
        ],
        compiler_params=pltpu.CompilerParams(collective_id=0, has_side_effects=True),
        name="gather_ops",
    )(packed, quad_weight, flat_density, rotation)
    blocks, partial = pl.pallas_call(
        functools.partial(pair_kernel, slots, grp, wide, rows),
        out_shape=(
            jax.ShapeDtypeStruct((slots, 3, 3, n, n), jnp.bfloat16),
            jax.ShapeDtypeStruct((grp, rows, lanes), jnp.float32),
        ),
        in_specs=[pl.BlockSpec(memory_space=pltpu.SMEM), vmem, vmem, vmem],
        out_specs=(any_space, vmem),
        scratch_shapes=[
            pltpu.VMEM((wide * slots, 6, n, 128), jnp.float32),
            pltpu.VMEM((lanes, 2 * rows), jnp.float32),
            pltpu.VMEM((grp * slots, 3, 8, lanes), jnp.float32),
            pltpu.VMEM((grp * slots, 3, 8, lanes), jnp.float32),
            pltpu.SMEM((grp * slots * wide * slots + 1,), jnp.int32),
            pltpu.SemaphoreType.DMA((9 * slots,)),
        ],
        name="pair_sums",
    )(flags, ops6, targets, sources)
    velocity = pl.pallas_call(
        functools.partial(scatter_kernel, slots, grp),
        out_shape=jax.ShapeDtypeStruct((3 * slots, n), jnp.float32),
        in_specs=[vmem] * 3,
        out_specs=vmem,
        scratch_shapes=[
            pltpu.VMEM((grp, rows, lanes), jnp.float32),
            pltpu.SemaphoreType.DMA((grp,)),
            pltpu.SemaphoreType.DMA((grp,)),
        ],
        compiler_params=pltpu.CompilerParams(collective_id=1, has_side_effects=True),
        name="scatter_sums",
    )(partial, self_velocity, packed[rows:])
    return (
        blocks.transpose(0, 1, 3, 2, 4),
        velocity.reshape(3, slots, n).transpose(1, 0, 2),
    )


def solution(mesh):
    placed = (
        P(("wide", "grp"), None, None),
        P(("wide", "grp"), None, None),
        P(("wide", "grp"), None),
        P(("wide", "grp")),
        P(("wide", "grp"), None),
        P(),
    )
    return jax.shard_map(
        on_device,
        mesh=mesh,
        in_specs=placed,
        out_specs=(P(("wide", "grp"), None, None, None, None), P(("wide", "grp"), None, None)),
        check_vma=False,
    )
```

```python
import functools
import jax
import jax.numpy as jnp
from jax import lax
from jax.experimental import pallas as pl
from jax.experimental.pallas import tpu as pltpu
from jax.sharding import PartitionSpec as P

soft_square = 0.0625
MESH = pl.DeviceIdType.MESH
SYM = ((0, 0), (0, 1), (0, 2), (1, 1), (1, 2), (2, 2))


def up(value, step):
    return (value + step - 1) // step * step


def split3(x):
    hi = x.astype(jnp.bfloat16)
    rest = x - hi.astype(jnp.float32)
    mid = rest.astype(jnp.bfloat16)
    low = (rest - mid.astype(jnp.float32)).astype(jnp.bfloat16)
    return hi, mid, low


def gather_kernel(
    slots, grp, wide, rows, chunk, stride,
    shape_ref, dens_ref, qw_ref, live_ref, nbr_ref, rot_ref,
    ops_ref, vel_ref, tgt_ref, src_ref, list_ref,
    own, mats, parts, gbuf, cbuf, kern, cols, table, sums, gsend, grecv, csend, crecv,
):
    n = rot_ref.shape[0]
    lanes = own.shape[1]
    span = parts.shape[2]
    caps = nbr_ref.shape[1]
    me_g = lax.axis_index("grp")
    me_w = lax.axis_index("wide")
    me = me_w * grp + me_g
    barrier = pltpu.get_barrier_semaphore()
    peers = [(dw, dg) for dw in range(wide) for dg in range(grp) if dw or dg]

    def place(dw, dg):
        return {"wide": lax.rem(me_w + dw, wide), "grp": lax.rem(me_g + dg, grp)}

    for dw, dg in peers:
        pl.semaphore_signal(barrier, inc=1, device_id=place(dw, dg), device_id_type=MESH)

    own[...] = jnp.zeros_like(own)
    mats[...] = jnp.zeros_like(mats)
    alive = [live_ref[c].astype(jnp.float32) for c in range(slots)]
    for c in range(slots):
        for a in range(3):
            row = shape_ref[a, c : c + 1, :]
            own[a * slots + c : a * slots + c + 1, 0:n] = row
            mats[c, a : a + 1, 0:n] = row
            mats[c, 3 + a : 4 + a, 0:n] = qw_ref[c : c + 1, :] * dens_ref[a, c : c + 1, :] * alive[c]
        own[3 * slots + c : 3 * slots + c + 1, 0:caps] = (
            nbr_ref[c : c + 1, :].astype(jnp.float32) * alive[c]
        )
    lane = lax.broadcasted_iota(jnp.int32, (8, span), 1)
    level = lax.broadcasted_iota(jnp.int32, (8, span), 0)
    tag = jnp.zeros((8, span), jnp.float32)
    for c in range(slots):
        tag = jnp.where(lane == me * slots + c, alive[c], tag)
    for g in range(grp):
        made = jnp.where(level == 6, tag, 0.0)
        for c in range(slots):
            moved = pltpu.roll(mats[c], (c * stride - g * chunk) % lanes, axis=1)[:, 0:span]
            inside = (lane >= c * stride) & (lane < c * stride + chunk) & (level < 6)
            made = jnp.where(inside, moved, made)
        parts[g] = made

    pl.semaphore_wait(barrier, len(peers))
    copies = []
    for dg in range(1, grp):
        copies.append(
            pltpu.make_async_remote_copy(
                src_ref=own,
                dst_ref=gbuf.at[me_g],
                send_sem=gsend.at[dg],
                recv_sem=grecv.at[dg],
                device_id=place(0, dg),
                device_id_type=MESH,
            )
        )
    for dw, dg in peers:
        copies.append(
            pltpu.make_async_remote_copy(
                src_ref=parts.at[lax.rem(me_g + dg, grp)],
                dst_ref=cbuf.at[me],
                send_sem=csend.at[dw * grp + dg],
                recv_sem=crecv.at[dw * grp + dg],
                device_id=place(dw, dg),
                device_id_type=MESH,
            )
        )
    for copy in copies:
        copy.start()

    rot = rot_ref[...]
    table[...] = jnp.zeros_like(table)
    table[:, 0:n] = rot
    few = lax.broadcasted_iota(jnp.int32, (n, 8), 1)
    tall = lax.broadcasted_iota(jnp.int32, (kern.shape[1], 8), 1)
    for c in range(slots):
        pos = jnp.concatenate([shape_ref[a, c : c + 1, :] for a in range(3)], axis=0)
        nodes = None
        for piece in split3(pos):
            part = lax.dot_general(
                piece, rot, (((1,), (1,)), ((), ())), preferred_element_type=jnp.float32
            )
            nodes = part if nodes is None else nodes + part
        weight = qw_ref[c : c + 1, :]
        cols[...] = jnp.transpose(mats[c])
        force = [dens_ref[b, c : c + 1, :] for b in range(3)]
        force = jnp.concatenate(force + force + [jnp.zeros((2, n), jnp.float32)], axis=0)
        force = jnp.concatenate([force, jnp.zeros((8, lanes - n), jnp.float32)], axis=1)
        turned = jnp.transpose(force)[0:n].astype(jnp.bfloat16)
        pushed = jnp.dot(rot, turned, preferred_element_type=jnp.float32)
        coarse = pushed.astype(jnp.bfloat16).astype(jnp.float32)
        table[:, lanes : lanes + 8] = jnp.where(few < 3, coarse, pushed - coarse).astype(jnp.bfloat16)

        def block_step(step, carry):
            start = pl.multiple_of(step * 16, 16)
            block = cols[pl.ds(start, 16), :]
            diff = [block[:, a : a + 1] - nodes[a : a + 1, :] for a in range(3)]
            dist = diff[0] * diff[0] + diff[1] * diff[1] + diff[2] * diff[2]
            inv = lax.rsqrt(dist + soft_square)
            scaled = inv * inv * inv * weight
            half = [d * scaled for d in diff]
            diag = (dist + 2.0 * soft_square) * scaled
            for index, (a, b) in enumerate(SYM):
                value = half[a] * diff[b]
                if a == b:
                    value = value + diag
                kern[index, pl.ds(start, 16), :] = value.astype(jnp.bfloat16)
            return carry

        steps = kern.shape[1] // 16
        lax.fori_loop(0, steps, block_step, 0, unroll=4 if steps % 4 == 0 else 1)
        total = [jnp.zeros((kern.shape[1], 8), jnp.float32) for _ in range(3)]
        for index, (a, b) in enumerate(SYM):
            product = jnp.dot(kern[index], table[...], preferred_element_type=jnp.float32)
            ops_ref[c, index] = jnp.where(alive[c] > 0.0, product[:n, :n], 0.0).astype(jnp.bfloat16)
            column = product[:, lanes : lanes + 8]
            total[a] = total[a] + jnp.where((tall == b) | (tall == 3 + b), column, 0.0)
            if a != b:
                total[b] = total[b] + jnp.where((tall == a) | (tall == 3 + a), column, 0.0)
        for a in range(3):
            sums[...] = jnp.zeros_like(sums)
            sums[0 : kern.shape[1], :] = total[a]
            row = jnp.sum(jnp.transpose(sums[...]), axis=0, keepdims=True)
            vel_ref[a, c : c + 1, :] = row[:, :n]

    gbuf[me_g] = own[...]
    cbuf[me] = parts[me_g]
    for copy in copies:
        copy.wait()
    tgt_ref[...] = gbuf[...]
    src_ref[...] = cbuf[...]
    group = grp * slots
    width = list_ref.shape[1]
    living = jnp.sum(cbuf[...], axis=0)[6:7, 0:width]
    wanted = jnp.concatenate(
        [gbuf[g, 3 * slots : 4 * slots, 0:width] for g in range(grp)], axis=0
    )
    slot_row = lax.broadcasted_iota(jnp.int32, (group, width), 0) + me_w * group
    slot_col = lax.broadcasted_iota(jnp.int32, (group, width), 1)
    wanted = jnp.where((wanted * living > 0.0) & (slot_row != slot_col), 1.0, 0.0)
    before = lax.broadcasted_iota(jnp.int32, (width, width), 0)
    after = lax.broadcasted_iota(jnp.int32, (width, width), 1)
    lower = jnp.where(before < after, 1.0, 0.0).astype(jnp.bfloat16)
    rank = jnp.dot(wanted.astype(jnp.bfloat16), lower, preferred_element_type=jnp.float32)
    rank = jnp.where(wanted > 0.0, rank, -1.0)
    rank_cols = jnp.transpose(rank)
    seat = lax.broadcasted_iota(jnp.int32, (caps, width), 1).astype(jnp.float32)
    name = (lax.broadcasted_iota(jnp.int32, (caps, width), 0) - caps).astype(jnp.float32)
    for t in range(group):
        here = jnp.where(rank_cols[0:caps, t : t + 1] == seat, name, 0.0)
        ids = jnp.sum(here, axis=0, keepdims=True) + caps
        list_ref[t : t + 1, :] = ids.astype(jnp.int32)
    counts = jnp.sum(wanted, axis=1, keepdims=True)
    list_ref[group : 2 * group, :] = jnp.broadcast_to(counts, (group, width)).astype(jnp.int32)
    list_ref[2 * group : 2 * group + 8, :] = jnp.broadcast_to(living, (8, width)).astype(jnp.int32)


def pair_kernel(
    slots, grp, wide, rows, stride,
    list_ref, ops_ref, tgt_ref, src_ref,
    out_ref, acc_ref, spread, flip, aim, heap, sems,
):
    lanes = tgt_ref.shape[2]
    group = grp * slots
    caps = wide * group
    copies = []
    for c in range(slots):
        for a in range(3):
            for b in range(3):
                index = SYM.index((min(a, b), max(a, b)))
                copies.append(
                    pltpu.make_async_copy(
                        ops_ref.at[c, index], out_ref.at[c, a, b], sems.at[len(copies)]
                    )
                )
    for copy in copies:
        copy.start()
    acc_ref[...] = jnp.zeros_like(acc_ref)
    for t in range(group):
        for a in range(3):
            row = a * slots + t % slots
            aim[t, a] = jnp.broadcast_to(tgt_ref[t // slots, row : row + 1, :], (8, lanes))
    spread[caps] = jnp.zeros_like(spread[caps])
    for lead in range(0, wide * grp, 16):
        many = min(16, wide * grp - lead)
        flip[:, 0 : many * 8] = jnp.transpose(
            src_ref[lead : lead + many].reshape(many * 8, src_ref.shape[2])
        )
        for near in range(many):
            for c in range(slots):
                slot = (lead + near) * slots + c

                @pl.when(list_ref[2 * group, slot] > 0)
                def _():
                    for k in range(6):
                        spread[slot, k] = jnp.broadcast_to(
                            flip[c * stride : c * stride + stride, near * 8 + k : near * 8 + k + 1],
                            (stride, 128),
                        )

    tiles = lanes // 128

    def one_target(t, carry):
        xs = [
            [aim[t, a, :, l * 128 : l * 128 + 128] for a in range(3)] for l in range(tiles)
        ]

        def step(p, sums):
            sums = list(sums)
            for half in range(2):
                s = list_ref[t, 2 * p + half]
                for j in range(0, stride, 8):
                    y = [spread[s, a, j : j + 8, :] for a in range(3)]
                    f = [spread[s, 3 + a, j : j + 8, :] for a in range(3)]
                    for l in range(tiles):
                        d = [xs[l][a] - y[a] for a in range(3)]
                        dist = (d[0] * d[0] + d[1] * d[1]) + d[2] * d[2] + soft_square
                        inv = lax.rsqrt(dist)
                        cube = inv * inv * inv
                        dot = d[0] * f[0] + d[1] * f[1] + d[2] * f[2]
                        near = (dist + soft_square) * cube
                        far = dot * cube
                        for a in range(3):
                            sums[l * 3 + a] = sums[l * 3 + a] + (f[a] * near + d[a] * far)
            return tuple(sums)

        zero = tuple(jnp.zeros((8, 128), jnp.float32) for _ in range(3 * tiles))
        sums = lax.fori_loop(0, (list_ref[group + t, 0] + 1) // 2, step, zero)
        for l in range(tiles):
            for a in range(3):
                heap[t, a, :, l * 128 : l * 128 + 128] = sums[l * 3 + a]
        return carry

    lax.fori_loop(0, group, one_target, 0)
    for t in range(group):
        for a in range(3):
            row = a * slots + t % slots
            acc_ref[t // slots, row : row + 1, :] = jnp.sum(heap[t, a], axis=0, keepdims=True)
    for copy in copies:
        copy.wait()


def scatter_kernel(slots, grp, part_ref, self_ref, live_ref, vel_ref, got, send, recv):
    n = self_ref.shape[2]
    me = lax.axis_index("grp")
    barrier = pltpu.get_barrier_semaphore()
    for off in range(1, grp):
        pl.semaphore_signal(
            barrier, inc=1, device_id={"grp": lax.rem(me + off, grp)}, device_id_type=MESH
        )
    pl.semaphore_wait(barrier, grp - 1)
    copies = []
    for off in range(1, grp):
        peer = lax.rem(me + off, grp)
        copies.append(
            pltpu.make_async_remote_copy(
                src_ref=part_ref.at[peer],
                dst_ref=got.at[off],
                send_sem=send.at[off],
                recv_sem=recv.at[off],
                device_id={"grp": peer},
                device_id_type=MESH,
            )
        )
    for copy in copies:
        copy.start()
    total = part_ref[me]
    for index, copy in enumerate(copies):
        copy.wait()
        total = total + got[index + 1]
    for a in range(3):
        for c in range(slots):
            row = a * slots + c
            value = self_ref[a, c : c + 1, :] + total[row : row + 1, :n]
            vel_ref[a, c : c + 1, :] = value * live_ref[c].astype(jnp.float32)


def on_device(shapes, density, quad_weight, live, neighbor, rotation):
    slots, _, n = shapes.shape
    caps = neighbor.shape[1]
    grp = lax.axis_size("grp")
    wide = lax.axis_size("wide")
    group = grp * slots
    rows = up(4 * slots, 8)
    lanes = up(max(n, caps), 128)
    width = up(caps, 128)
    tall = up(n, 16)
    chunk = -(-n // grp)
    stride = up(chunk, 8)
    span = max(width, up(slots * stride, 128))
    flat_shapes = shapes.transpose(1, 0, 2)
    flat_density = density.transpose(1, 0, 2)
    vmem = pl.BlockSpec(memory_space=pltpu.VMEM)
    smem = pl.BlockSpec(memory_space=pltpu.SMEM)
    any_space = pl.BlockSpec(memory_space=pl.ANY)
    ops6, self_velocity, targets, sources, lists = pl.pallas_call(
        functools.partial(gather_kernel, slots, grp, wide, rows, chunk, stride),
        out_shape=(
            jax.ShapeDtypeStruct((slots, 6, n, n), jnp.bfloat16),
            jax.ShapeDtypeStruct((3, slots, n), jnp.float32),
            jax.ShapeDtypeStruct((grp, rows, lanes), jnp.float32),
            jax.ShapeDtypeStruct((wide * grp, 8, span), jnp.float32),
            jax.ShapeDtypeStruct((2 * group + 8, width), jnp.int32),
        ),
        in_specs=[vmem, vmem, vmem, smem, vmem, vmem],
        out_specs=(vmem,) * 5,
        scratch_shapes=[
            pltpu.VMEM((rows, lanes), jnp.float32),
            pltpu.VMEM((slots, 8, lanes), jnp.float32),
            pltpu.VMEM((grp, 8, span), jnp.float32),
            pltpu.VMEM((grp, rows, lanes), jnp.float32),
            pltpu.VMEM((wide * grp, 8, span), jnp.float32),
            pltpu.VMEM((6, tall, n), jnp.bfloat16),
            pltpu.VMEM((lanes, 8), jnp.float32),
            pltpu.VMEM((n, lanes + 8), jnp.bfloat16),
            pltpu.VMEM((lanes, 8), jnp.float32),
            pltpu.SemaphoreType.DMA((grp,)),
            pltpu.SemaphoreType.DMA((grp,)),
            pltpu.SemaphoreType.DMA((wide * grp,)),
            pltpu.SemaphoreType.DMA((wide * grp,)),
        ],
        compiler_params=pltpu.CompilerParams(collective_id=0, has_side_effects=True),
        name="gather_ops",
    )(flat_shapes, flat_density, quad_weight, live, neighbor, rotation)
    blocks, partial = pl.pallas_call(
        functools.partial(pair_kernel, slots, grp, wide, rows, stride),
        out_shape=(
            jax.ShapeDtypeStruct((slots, 3, 3, n, n), jnp.bfloat16),
            jax.ShapeDtypeStruct((grp, rows, lanes), jnp.float32),
        ),
        in_specs=[smem, vmem, vmem, vmem],
        out_specs=(any_space, vmem),
        scratch_shapes=[
            pltpu.VMEM((caps + 1, 6, stride, 128), jnp.float32),
            pltpu.VMEM((span, 128), jnp.float32),
            pltpu.VMEM((group, 3, 8, lanes), jnp.float32),
            pltpu.VMEM((group, 3, 8, lanes), jnp.float32),
            pltpu.SemaphoreType.DMA((9 * slots,)),
        ],
        name="pair_sums",
    )(lists, ops6, targets, sources)
    velocity = pl.pallas_call(
        functools.partial(scatter_kernel, slots, grp),
        out_shape=jax.ShapeDtypeStruct((3, slots, n), jnp.float32),
        in_specs=[vmem, vmem, smem],
        out_specs=vmem,
        scratch_shapes=[
            pltpu.VMEM((grp, rows, lanes), jnp.float32),
            pltpu.SemaphoreType.DMA((grp,)),
            pltpu.SemaphoreType.DMA((grp,)),
        ],
        compiler_params=pltpu.CompilerParams(collective_id=1, has_side_effects=True),
        name="scatter_sums",
    )(partial, self_velocity, live)
    return (blocks.transpose(0, 1, 3, 2, 4), velocity.transpose(1, 0, 2))


def solution(mesh):
    placed = (
        P(("wide", "grp"), None, None),
        P(("wide", "grp"), None, None),
        P(("wide", "grp"), None),
        P(("wide", "grp")),
        P(("wide", "grp"), None),
        P(),
    )
    return jax.shard_map(
        on_device,
        mesh=mesh,
        in_specs=placed,
        out_specs=(P(("wide", "grp"), None, None, None, None), P(("wide", "grp"), None, None)),
        check_vma=False,
    )
```

```python
import functools
import jax
import jax.numpy as jnp
from jax import lax
from jax.experimental import pallas as pl
from jax.experimental.pallas import tpu as pltpu
from jax.sharding import PartitionSpec as P

soft_square = 0.0625
MESH = pl.DeviceIdType.MESH
SYM = ((0, 0), (0, 1), (0, 2), (1, 1), (1, 2), (2, 2))


def up(value, step):
    return (value + step - 1) // step * step


def split3(x):
    hi = x.astype(jnp.bfloat16)
    rest = x - hi.astype(jnp.float32)
    mid = rest.astype(jnp.bfloat16)
    low = (rest - mid.astype(jnp.float32)).astype(jnp.bfloat16)
    return hi, mid, low


def gather_kernel(
    slots, grp, wide, rows, chunk, stride, packs,
    shape_ref, dens_ref, qw_ref, live_ref, nbr_ref, rot_ref,
    ops_ref, vel_ref, tgt_ref, src_ref, list_ref,
    ops_buf, ops_sem, own, mats, parts, gbuf, cbuf, kern, cols, table, sums, gsend, grecv, csend, crecv,
):
    n = rot_ref.shape[0]
    lanes = own.shape[1]
    span = parts.shape[2]
    caps = nbr_ref.shape[1]
    me_g = lax.axis_index("grp")
    me_w = lax.axis_index("wide")
    me = me_w * grp + me_g
    barrier = pltpu.get_barrier_semaphore()
    peers = [(dw, dg) for dw in range(wide) for dg in range(grp) if dw or dg]

    def place(dw, dg):
        return {"wide": lax.rem(me_w + dw, wide), "grp": lax.rem(me_g + dg, grp)}

    for dw, dg in peers:
        pl.semaphore_signal(barrier, inc=1, device_id=place(dw, dg), device_id_type=MESH)

    own[...] = jnp.zeros_like(own)
    mats[...] = jnp.zeros_like(mats)
    alive = [live_ref[c].astype(jnp.float32) for c in range(slots)]
    for c in range(slots):
        for a in range(3):
            row = shape_ref[a, c : c + 1, :]
            own[a * slots + c : a * slots + c + 1, 0:n] = row
            mats[c, a : a + 1, 0:n] = row
            mats[c, 3 + a : 4 + a, 0:n] = qw_ref[c : c + 1, :] * dens_ref[a, c : c + 1, :] * alive[c]
        own[3 * slots + c : 3 * slots + c + 1, 0:caps] = (
            nbr_ref[c : c + 1, :].astype(jnp.float32) * alive[c]
        )
    lane = lax.broadcasted_iota(jnp.int32, (1, span), 1)
    tag = jnp.zeros((1, span), jnp.float32)
    for c in range(slots):
        tag = jnp.where(lane == packs * stride + c, alive[c], tag)
    for g in range(grp):
        for r in range(parts.shape[1]):
            made = tag
            for q in range(packs):
                c, k = divmod(r * packs + q, 6)
                if c < slots:
                    moved = pltpu.roll(mats[c], (q * stride - g * chunk) % lanes, axis=1)
                    inside = (lane >= q * stride) & (lane < q * stride + chunk)
                    made = jnp.where(inside, moved[k : k + 1, 0:span], made)
            parts[g, r : r + 1, :] = made

    pl.semaphore_wait(barrier, len(peers))
    copies = []
    for dg in range(1, grp):
        copies.append(
            pltpu.make_async_remote_copy(
                src_ref=own,
                dst_ref=gbuf.at[me_g],
                send_sem=gsend.at[dg],
                recv_sem=grecv.at[dg],
                device_id=place(0, dg),
                device_id_type=MESH,
            )
        )
    for dw, dg in peers:
        copies.append(
            pltpu.make_async_remote_copy(
                src_ref=parts.at[lax.rem(me_g + dg, grp)],
                dst_ref=cbuf.at[me],
                send_sem=csend.at[dw * grp + dg],
                recv_sem=crecv.at[dw * grp + dg],
                device_id=place(dw, dg),
                device_id_type=MESH,
            )
        )
    for copy in copies:
        copy.start()

    rot = rot_ref[...]
    table[...] = jnp.zeros_like(table)
    table[:, 0:n] = rot
    few = lax.broadcasted_iota(jnp.int32, (n, 8), 1)
    tall = lax.broadcasted_iota(jnp.int32, (kern.shape[1], 8), 1)
    for c in range(slots):
        pos = jnp.concatenate([shape_ref[a, c : c + 1, :] for a in range(3)], axis=0)
        nodes = None
        for piece in split3(pos):
            part = lax.dot_general(
                piece, rot, (((1,), (1,)), ((), ())), preferred_element_type=jnp.float32
            )
            nodes = part if nodes is None else nodes + part
        weight = qw_ref[c : c + 1, :]
        cols[...] = jnp.transpose(mats[c])
        force = [dens_ref[b, c : c + 1, :] for b in range(3)]
        force = jnp.concatenate(force + force + [jnp.zeros((2, n), jnp.float32)], axis=0)
        force = jnp.concatenate([force, jnp.zeros((8, lanes - n), jnp.float32)], axis=1)
        turned = jnp.transpose(force)[0:n].astype(jnp.bfloat16)
        pushed = jnp.dot(rot, turned, preferred_element_type=jnp.float32)
        coarse = pushed.astype(jnp.bfloat16).astype(jnp.float32)
        table[:, lanes : lanes + 8] = jnp.where(few < 3, coarse, pushed - coarse).astype(jnp.bfloat16)

        def block_step(step, carry):
            start = pl.multiple_of(step * 16, 16)
            block = cols[pl.ds(start, 16), :]
            diff = [block[:, a : a + 1] - nodes[a : a + 1, :] for a in range(3)]
            dist = diff[0] * diff[0] + diff[1] * diff[1] + diff[2] * diff[2]
            inv = lax.rsqrt(dist + soft_square)
            scaled = inv * inv * inv * weight
            half = [d * scaled for d in diff]
            diag = (dist + 2.0 * soft_square) * scaled
            for index, (a, b) in enumerate(SYM):
                value = half[a] * diff[b]
                if a == b:
                    value = value + diag
                kern[index, pl.ds(start, 16), :] = value.astype(jnp.bfloat16)
            return carry

        steps = kern.shape[1] // 16
        lax.fori_loop(0, steps, block_step, 0, unroll=4 if steps % 4 == 0 else 1)
        total = [jnp.zeros((kern.shape[1], 8), jnp.float32) for _ in range(3)]
        for index, (a, b) in enumerate(SYM):
            product = jnp.dot(kern[index], table[...], preferred_element_type=jnp.float32)
            ops_buf[c, index] = jnp.where(alive[c] > 0.0, product[:n, :n], 0.0).astype(jnp.bfloat16)
            column = product[:, lanes : lanes + 8]
            total[a] = total[a] + jnp.where((tall == b) | (tall == 3 + b), column, 0.0)
            if a != b:
                total[b] = total[b] + jnp.where((tall == a) | (tall == 3 + a), column, 0.0)
        for a in range(3):
            sums[...] = jnp.zeros_like(sums)
            sums[0 : kern.shape[1], :] = total[a]
            row = jnp.sum(jnp.transpose(sums[...]), axis=0, keepdims=True)
            vel_ref[a, c : c + 1, :] = row[:, :n]
        store = pltpu.make_async_copy(ops_buf.at[c], ops_ref.at[c], ops_sem.at[c])
        store.start()
        copies.append(store)

    gbuf[me_g] = own[...]
    cbuf[me] = parts[me_g]
    for copy in copies:
        copy.wait()
    tgt_ref[...] = gbuf[...]
    depth = cbuf.shape[1]
    for d in range(wide * grp):
        src_ref[d * depth : d * depth + depth, :] = cbuf[d]
    group = grp * slots
    width = list_ref.shape[1]
    first = jnp.concatenate([cbuf[d, 0:1, :] for d in range(wide * grp)], axis=0)
    source_row = lax.broadcasted_iota(jnp.int32, (wide * grp, width), 0)
    source_col = lax.broadcasted_iota(jnp.int32, (wide * grp, width), 1)
    living = jnp.zeros((1, width), jnp.float32)
    for c in range(slots):
        flag = first[:, packs * stride + c : packs * stride + c + 1]
        living = living + jnp.sum(
            jnp.where(source_col == source_row * slots + c, flag, 0.0), axis=0, keepdims=True
        )
    wanted = jnp.concatenate(
        [gbuf[g, 3 * slots : 4 * slots, 0:width] for g in range(grp)], axis=0
    )
    slot_row = lax.broadcasted_iota(jnp.int32, (group, width), 0) + me_w * group
    slot_col = lax.broadcasted_iota(jnp.int32, (group, width), 1)
    wanted = jnp.where((wanted * living > 0.0) & (slot_row != slot_col), 1.0, 0.0)
    before = lax.broadcasted_iota(jnp.int32, (width, width), 0)
    after = lax.broadcasted_iota(jnp.int32, (width, width), 1)
    lower = jnp.where(before < after, 1.0, 0.0).astype(jnp.bfloat16)
    rank = jnp.dot(wanted.astype(jnp.bfloat16), lower, preferred_element_type=jnp.float32)
    rank = jnp.where(wanted > 0.0, rank, -1.0)
    rank_cols = jnp.transpose(rank)
    seat = lax.broadcasted_iota(jnp.int32, (caps, width), 1).astype(jnp.float32)
    name = (lax.broadcasted_iota(jnp.int32, (caps, width), 0) - caps).astype(jnp.float32)
    for t in range(group):
        here = jnp.where(rank_cols[0:caps, t : t + 1] == seat, name, 0.0)
        ids = jnp.sum(here, axis=0, keepdims=True) + caps
        list_ref[t : t + 1, :] = ids.astype(jnp.int32)
    counts = jnp.sum(wanted, axis=1, keepdims=True)
    list_ref[group : 2 * group, :] = jnp.broadcast_to(counts, (group, width)).astype(jnp.int32)
    list_ref[2 * group : 2 * group + 8, :] = jnp.broadcast_to(living, (8, width)).astype(jnp.int32)


def pair_kernel(
    slots, grp, wide, rows, stride, packs,
    list_ref, ops_ref, tgt_ref, src_ref,
    out_ref, acc_ref, ops_buf, ops_sem, spread, flip, aim, heap, sems,
):
    lanes = tgt_ref.shape[2]
    group = grp * slots
    caps = wide * group
    loads = [
        pltpu.make_async_copy(ops_ref.at[c], ops_buf.at[c], ops_sem.at[c]) for c in range(slots)
    ]
    for load in loads:
        load.start()
    copies = []
    for c in range(slots):
        for a in range(3):
            for b in range(3):
                index = SYM.index((min(a, b), max(a, b)))
                copies.append(
                    pltpu.make_async_copy(
                        ops_buf.at[c, index], out_ref.at[c, a, b], sems.at[len(copies)]
                    )
                )
    for t in range(group):
        for a in range(3):
            row = a * slots + t % slots
            aim[t, a] = jnp.broadcast_to(tgt_ref[t // slots, row : row + 1, :], (8, lanes))
    spread[caps] = jnp.zeros_like(spread[caps])
    depth = src_ref.shape[0] // (wide * grp)
    batch = 128 // up(depth, 4)
    for lead in range(0, wide * grp, batch):
        many = min(batch, wide * grp - lead)
        flip[:, 0 : many * depth] = jnp.transpose(src_ref[lead * depth : (lead + many) * depth, :])
        for near in range(many):
            for c in range(slots):
                slot = (lead + near) * slots + c

                @pl.when(list_ref[2 * group, slot] > 0)
                def _():
                    for k in range(6):
                        r, q = divmod(c * 6 + k, packs)
                        column = near * depth + r
                        spread[slot, k] = jnp.broadcast_to(
                            flip[q * stride : q * stride + stride, column : column + 1],
                            (stride, 128),
                        )

    for load in loads:
        load.wait()
    for copy in copies:
        copy.start()
    tiles = lanes // 128

    def one_target(t, carry):
        xs = [
            [aim[t, a, :, l * 128 : l * 128 + 128] for a in range(3)] for l in range(tiles)
        ]

        def step(p, sums):
            sums = list(sums)
            for half in range(2):
                s = list_ref[t, 2 * p + half]
                for j in range(0, stride, 8):
                    y = [spread[s, a, j : j + 8, :] for a in range(3)]
                    f = [spread[s, 3 + a, j : j + 8, :] for a in range(3)]
                    for l in range(tiles):
                        d = [xs[l][a] - y[a] for a in range(3)]
                        dist = (d[0] * d[0] + d[1] * d[1]) + d[2] * d[2] + soft_square
                        inv = lax.rsqrt(dist)
                        cube = inv * inv * inv
                        dot = d[0] * f[0] + d[1] * f[1] + d[2] * f[2]
                        near = (dist + soft_square) * cube
                        far = dot * cube
                        for a in range(3):
                            sums[l * 3 + a] = sums[l * 3 + a] + (f[a] * near + d[a] * far)
            return tuple(sums)

        zero = tuple(jnp.zeros((8, 128), jnp.float32) for _ in range(3 * tiles))
        sums = lax.fori_loop(0, (list_ref[group + t, 0] + 1) // 2, step, zero)
        for l in range(tiles):
            for a in range(3):
                heap[t, a, :, l * 128 : l * 128 + 128] = sums[l * 3 + a]
        return carry

    lax.fori_loop(0, group, one_target, 0)
    for t in range(group):
        for a in range(3):
            row = (a * slots + t % slots) * tiles
            whole = jnp.sum(heap[t, a], axis=0, keepdims=True)
            for l in range(tiles):
                acc_ref[t // slots, row + l : row + l + 1, :] = whole[:, l * 128 : l * 128 + 128]
    for copy in copies:
        copy.wait()


def scatter_kernel(slots, grp, part_ref, self_ref, live_ref, vel_ref, got, send, recv):
    n = self_ref.shape[2]
    tiles = part_ref.shape[1] // (3 * slots)
    me = lax.axis_index("grp")
    barrier = pltpu.get_barrier_semaphore()
    for off in range(1, grp):
        pl.semaphore_signal(
            barrier, inc=1, device_id={"grp": lax.rem(me + off, grp)}, device_id_type=MESH
        )
    pl.semaphore_wait(barrier, grp - 1)
    copies = []
    for off in range(1, grp):
        peer = lax.rem(me + off, grp)
        copies.append(
            pltpu.make_async_remote_copy(
                src_ref=part_ref.at[peer],
                dst_ref=got.at[off],
                send_sem=send.at[off],
                recv_sem=recv.at[off],
                device_id={"grp": peer},
                device_id_type=MESH,
            )
        )
    for copy in copies:
        copy.start()
    total = part_ref[me]
    for index, copy in enumerate(copies):
        copy.wait()
        total = total + got[index + 1]
    for a in range(3):
        for c in range(slots):
            row = (a * slots + c) * tiles
            line = jnp.concatenate([total[row + l : row + l + 1] for l in range(tiles)], axis=1)
            value = self_ref[a, c : c + 1, :] + line[:, :n]
            vel_ref[a, c : c + 1, :] = value * live_ref[c].astype(jnp.float32)


def on_device(shapes, density, quad_weight, live, neighbor, rotation):
    slots, _, n = shapes.shape
    caps = neighbor.shape[1]
    grp = lax.axis_size("grp")
    wide = lax.axis_size("wide")
    group = grp * slots
    rows = up(4 * slots, 8)
    lanes = up(max(n, caps), 128)
    width = up(caps, 128)
    tall = up(n, 16)
    chunk = -(-n // grp)
    stride = up(chunk, 8)
    span = 128
    packs = (span - slots) // stride
    depth = -(-6 * slots // packs)
    flat_shapes = shapes.transpose(1, 0, 2)
    flat_density = density.transpose(1, 0, 2)
    vmem = pl.BlockSpec(memory_space=pltpu.VMEM)
    smem = pl.BlockSpec(memory_space=pltpu.SMEM)
    any_space = pl.BlockSpec(memory_space=pl.ANY)
    ops6, self_velocity, targets, sources, lists = pl.pallas_call(
        functools.partial(gather_kernel, slots, grp, wide, rows, chunk, stride, packs),
        out_shape=(
            jax.ShapeDtypeStruct((slots, 6, n, n), jnp.bfloat16),
            jax.ShapeDtypeStruct((3, slots, n), jnp.float32),
            jax.ShapeDtypeStruct((grp, rows, lanes), jnp.float32),
            jax.ShapeDtypeStruct((wide * grp * depth, span), jnp.float32),
            jax.ShapeDtypeStruct((2 * group + 8, width), jnp.int32),
        ),
        in_specs=[vmem, vmem, vmem, smem, vmem, vmem],
        out_specs=(any_space,) + (vmem,) * 4,
        scratch_shapes=[
            pltpu.VMEM((slots, 6, n, n), jnp.bfloat16),
            pltpu.SemaphoreType.DMA((slots,)),
            pltpu.VMEM((rows, lanes), jnp.float32),
            pltpu.VMEM((slots, 8, lanes), jnp.float32),
            pltpu.VMEM((grp, depth, span), jnp.float32),
            pltpu.VMEM((grp, rows, lanes), jnp.float32),
            pltpu.VMEM((wide * grp, depth, span), jnp.float32),
            pltpu.VMEM((6, tall, n), jnp.bfloat16),
            pltpu.VMEM((lanes, 8), jnp.float32),
            pltpu.VMEM((n, lanes + 8), jnp.bfloat16),
            pltpu.VMEM((lanes, 8), jnp.float32),
            pltpu.SemaphoreType.DMA((grp,)),
            pltpu.SemaphoreType.DMA((grp,)),
            pltpu.SemaphoreType.DMA((wide * grp,)),
            pltpu.SemaphoreType.DMA((wide * grp,)),
        ],
        compiler_params=pltpu.CompilerParams(collective_id=0, has_side_effects=True),
        name="gather_ops",
    )(flat_shapes, flat_density, quad_weight, live, neighbor, rotation)
    blocks, partial = pl.pallas_call(
        functools.partial(pair_kernel, slots, grp, wide, rows, stride, packs),
        out_shape=(
            jax.ShapeDtypeStruct((slots, 3, 3, n, n), jnp.bfloat16),
            jax.ShapeDtypeStruct((grp, 3 * slots * lanes // 128, 128), jnp.float32),
        ),
        in_specs=[smem, any_space, vmem, vmem],
        out_specs=(any_space, vmem),
        scratch_shapes=[
            pltpu.VMEM((slots, 6, n, n), jnp.bfloat16),
            pltpu.SemaphoreType.DMA((slots,)),
            pltpu.VMEM((caps + 1, 6, stride, 128), jnp.float32),
            pltpu.VMEM((span, 128), jnp.float32),
            pltpu.VMEM((group, 3, 8, lanes), jnp.float32),
            pltpu.VMEM((group, 3, 8, lanes), jnp.float32),
            pltpu.SemaphoreType.DMA((9 * slots,)),
        ],
        name="pair_sums",
    )(lists, ops6, targets, sources)
    velocity = pl.pallas_call(
        functools.partial(scatter_kernel, slots, grp),
        out_shape=jax.ShapeDtypeStruct((3, slots, n), jnp.float32),
        in_specs=[vmem, vmem, smem],
        out_specs=vmem,
        scratch_shapes=[
            pltpu.VMEM((grp, 3 * slots * lanes // 128, 128), jnp.float32),
            pltpu.SemaphoreType.DMA((grp,)),
            pltpu.SemaphoreType.DMA((grp,)),
        ],
        compiler_params=pltpu.CompilerParams(collective_id=1, has_side_effects=True),
        name="scatter_sums",
    )(partial, self_velocity, live)
    return (blocks.transpose(0, 1, 3, 2, 4), velocity.transpose(1, 0, 2))


def solution(mesh):
    placed = (
        P(("wide", "grp"), None, None),
        P(("wide", "grp"), None, None),
        P(("wide", "grp"), None),
        P(("wide", "grp")),
        P(("wide", "grp"), None),
        P(),
    )
    return jax.shard_map(
        on_device,
        mesh=mesh,
        in_specs=placed,
        out_specs=(P(("wide", "grp"), None, None, None, None), P(("wide", "grp"), None, None)),
        check_vma=False,
    )
```

```python
import functools
import jax
import jax.numpy as jnp
from jax import lax
from jax.experimental import pallas as pl
from jax.experimental.pallas import tpu as pltpu
from jax.sharding import PartitionSpec as P

soft_square = 0.0625
MESH = pl.DeviceIdType.MESH
SYM = ((0, 0), (0, 1), (0, 2), (1, 1), (1, 2), (2, 2))


def up(value, step):
    return (value + step - 1) // step * step


def split3(x):
    hi = x.astype(jnp.bfloat16)
    rest = x - hi.astype(jnp.float32)
    mid = rest.astype(jnp.bfloat16)
    low = (rest - mid.astype(jnp.float32)).astype(jnp.bfloat16)
    return hi, mid, low


def gather_kernel(
    slots, grp, wide, rows, chunk, stride, packs,
    shape_ref, dens_ref, qw_ref, live_ref, nbr_ref, rot_ref,
    ops_ref, vel_ref, tgt_ref, src_ref, list_ref,
    ops_buf, ops_sem, own, mats, parts, gbuf, cbuf, kern, cols, table, sums, gsend, grecv, csend, crecv,
):
    n = rot_ref.shape[0]
    lanes = own.shape[1]
    span = parts.shape[2]
    caps = nbr_ref.shape[1]
    me_g = lax.axis_index("grp")
    me_w = lax.axis_index("wide")
    me = me_w * grp + me_g
    barrier = pltpu.get_barrier_semaphore()
    peers = [(dw, dg) for dw in range(wide) for dg in range(grp) if dw or dg]

    def place(dw, dg):
        return {"wide": lax.rem(me_w + dw, wide), "grp": lax.rem(me_g + dg, grp)}

    for dw, dg in peers:
        pl.semaphore_signal(barrier, inc=1, device_id=place(dw, dg), device_id_type=MESH)

    own[...] = jnp.zeros_like(own)
    mats[...] = jnp.zeros_like(mats)
    alive = [live_ref[c].astype(jnp.float32) for c in range(slots)]
    for c in range(slots):
        for a in range(3):
            row = shape_ref[a, c : c + 1, :]
            own[a * slots + c : a * slots + c + 1, 0:n] = row
            mats[c, a : a + 1, 0:n] = row
            mats[c, 3 + a : 4 + a, 0:n] = qw_ref[c : c + 1, :] * dens_ref[a, c : c + 1, :] * alive[c]
        own[3 * slots + c : 3 * slots + c + 1, 0:caps] = (
            nbr_ref[c : c + 1, :].astype(jnp.float32) * alive[c]
        )
    lane = lax.broadcasted_iota(jnp.int32, (1, span), 1)
    tag = jnp.zeros((1, span), jnp.float32)
    for c in range(slots):
        tag = jnp.where(lane == packs * stride + c, alive[c], tag)
    for g in range(grp):
        for r in range(parts.shape[1]):
            made = tag
            for q in range(packs):
                c, k = divmod(r * packs + q, 6)
                if c < slots:
                    moved = pltpu.roll(mats[c], (q * stride - g * chunk) % lanes, axis=1)
                    inside = (lane >= q * stride) & (lane < q * stride + chunk)
                    made = jnp.where(inside, moved[k : k + 1, 0:span], made)
            parts[g, r : r + 1, :] = made

    pl.semaphore_wait(barrier, len(peers))
    copies = []
    for dg in range(1, grp):
        copies.append(
            pltpu.make_async_remote_copy(
                src_ref=own,
                dst_ref=gbuf.at[me_g],
                send_sem=gsend.at[dg],
                recv_sem=grecv.at[dg],
                device_id=place(0, dg),
                device_id_type=MESH,
            )
        )
    for dw, dg in peers:
        copies.append(
            pltpu.make_async_remote_copy(
                src_ref=parts.at[lax.rem(me_g + dg, grp)],
                dst_ref=cbuf.at[me],
                send_sem=csend.at[dw * grp + dg],
                recv_sem=crecv.at[dw * grp + dg],
                device_id=place(dw, dg),
                device_id_type=MESH,
            )
        )
    for copy in copies:
        copy.start()

    rot = rot_ref[...]
    table[...] = jnp.zeros_like(table)
    table[:, 0:n] = rot
    few = lax.broadcasted_iota(jnp.int32, (n, 8), 1)
    tall = lax.broadcasted_iota(jnp.int32, (kern.shape[1], 8), 1)
    for c in range(slots):
        pos = jnp.concatenate([shape_ref[a, c : c + 1, :] for a in range(3)], axis=0)
        nodes = None
        for piece in split3(pos):
            part = lax.dot_general(
                piece, rot, (((1,), (1,)), ((), ())), preferred_element_type=jnp.float32
            )
            nodes = part if nodes is None else nodes + part
        weight = qw_ref[c : c + 1, :]
        cols[...] = jnp.transpose(mats[c])
        force = [dens_ref[b, c : c + 1, :] for b in range(3)]
        force = jnp.concatenate(force + force + [jnp.zeros((2, n), jnp.float32)], axis=0)
        force = jnp.concatenate([force, jnp.zeros((8, lanes - n), jnp.float32)], axis=1)
        turned = jnp.transpose(force)[0:n].astype(jnp.bfloat16)
        pushed = jnp.dot(rot, turned, preferred_element_type=jnp.float32)
        coarse = pushed.astype(jnp.bfloat16).astype(jnp.float32)
        table[:, lanes : lanes + 8] = jnp.where(few < 3, coarse, pushed - coarse).astype(jnp.bfloat16)

        def block_step(step, carry):
            start = pl.multiple_of(step * 16, 16)
            block = cols[pl.ds(start, 16), :]
            diff = [block[:, a : a + 1] - nodes[a : a + 1, :] for a in range(3)]
            dist = diff[0] * diff[0] + diff[1] * diff[1] + diff[2] * diff[2]
            inv = lax.rsqrt(dist + soft_square)
            scaled = inv * inv * inv * weight
            half = [d * scaled for d in diff]
            diag = (dist + 2.0 * soft_square) * scaled
            for index, (a, b) in enumerate(SYM):
                value = half[a] * diff[b]
                if a == b:
                    value = value + diag
                kern[index, pl.ds(start, 16), :] = value.astype(jnp.bfloat16)
            return carry

        steps = kern.shape[1] // 16
        lax.fori_loop(0, steps, block_step, 0, unroll=4 if steps % 4 == 0 else 1)
        total = [jnp.zeros((kern.shape[1], 8), jnp.float32) for _ in range(3)]
        for index, (a, b) in enumerate(SYM):
            product = jnp.dot(kern[index], table[...], preferred_element_type=jnp.float32)
            ops_buf[c, index] = jnp.where(alive[c] > 0.0, product[:n, :n], 0.0).astype(jnp.bfloat16)
            column = product[:, lanes : lanes + 8]
            total[a] = total[a] + jnp.where((tall == b) | (tall == 3 + b), column, 0.0)
            if a != b:
                total[b] = total[b] + jnp.where((tall == a) | (tall == 3 + a), column, 0.0)
        for a in range(3):
            sums[...] = jnp.zeros_like(sums)
            sums[0 : kern.shape[1], :] = total[a]
            row = jnp.sum(jnp.transpose(sums[...]), axis=0, keepdims=True)
            vel_ref[a, c : c + 1, :] = row[:, :n]
        store = pltpu.make_async_copy(ops_buf.at[c], ops_ref.at[c], ops_sem.at[c])
        store.start()
        copies.append(store)

    gbuf[me_g] = own[...]
    cbuf[me] = parts[me_g]
    for copy in copies:
        copy.wait()
    tgt_ref[...] = gbuf[...]
    depth = cbuf.shape[1]
    for d in range(wide * grp):
        src_ref[d * depth : d * depth + depth, :] = cbuf[d]
    group = grp * slots
    width = list_ref.shape[1]
    first = jnp.concatenate([cbuf[d, 0:1, :] for d in range(wide * grp)], axis=0)
    source_row = lax.broadcasted_iota(jnp.int32, (wide * grp, width), 0)
    source_col = lax.broadcasted_iota(jnp.int32, (wide * grp, width), 1)
    living = jnp.zeros((1, width), jnp.float32)
    for c in range(slots):
        flag = first[:, packs * stride + c : packs * stride + c + 1]
        living = living + jnp.sum(
            jnp.where(source_col == source_row * slots + c, flag, 0.0), axis=0, keepdims=True
        )
    wanted = jnp.concatenate(
        [gbuf[g, 3 * slots : 4 * slots, 0:width] for g in range(grp)], axis=0
    )
    slot_row = lax.broadcasted_iota(jnp.int32, (group, width), 0) + me_w * group
    slot_col = lax.broadcasted_iota(jnp.int32, (group, width), 1)
    wanted = jnp.where((wanted * living > 0.0) & (slot_row != slot_col), 1.0, 0.0)
    before = lax.broadcasted_iota(jnp.int32, (width, width), 0)
    after = lax.broadcasted_iota(jnp.int32, (width, width), 1)
    lower = jnp.where(before < after, 1.0, 0.0).astype(jnp.bfloat16)
    rank = jnp.dot(wanted.astype(jnp.bfloat16), lower, preferred_element_type=jnp.float32)
    rank = jnp.where(wanted > 0.0, rank, -1.0)
    rank_cols = jnp.transpose(rank)
    seat = lax.broadcasted_iota(jnp.int32, (caps, width), 1).astype(jnp.float32)
    name = (lax.broadcasted_iota(jnp.int32, (caps, width), 0) - caps).astype(jnp.float32)
    for t in range(group):
        here = jnp.where(rank_cols[0:caps, t : t + 1] == seat, name, 0.0)
        ids = jnp.sum(here, axis=0, keepdims=True) + caps
        list_ref[t : t + 1, :] = ids.astype(jnp.int32)
    counts = jnp.sum(wanted, axis=1, keepdims=True)
    list_ref[group : 2 * group, :] = jnp.broadcast_to(counts, (group, width)).astype(jnp.int32)
    list_ref[2 * group : 2 * group + 8, :] = jnp.broadcast_to(living, (8, width)).astype(jnp.int32)


def pair_kernel(
    slots, grp, wide, rows, stride, packs,
    list_ref, ops_ref, tgt_ref, src_ref,
    out_ref, acc_ref, acc, ops_buf, ops_sem, spread, flip, aim, heap, sems,
):
    lanes = tgt_ref.shape[2]
    group = grp * slots
    caps = wide * group
    loads = [
        pltpu.make_async_copy(ops_ref.at[c], ops_buf.at[c], ops_sem.at[c]) for c in range(slots)
    ]
    for load in loads:
        load.start()
    copies = []
    for c in range(slots):
        for a in range(3):
            for b in range(3):
                index = SYM.index((min(a, b), max(a, b)))
                copies.append(
                    pltpu.make_async_copy(
                        ops_buf.at[c, index], out_ref.at[c, a, b], sems.at[len(copies)]
                    )
                )
    for t in range(group):
        for a in range(3):
            row = a * slots + t % slots
            aim[t, a] = jnp.broadcast_to(tgt_ref[t // slots, row : row + 1, :], (8, lanes))
    spread[caps] = jnp.zeros_like(spread[caps])
    depth = src_ref.shape[0] // (wide * grp)
    batch = 128 // up(depth, 4)
    for lead in range(0, wide * grp, batch):
        many = min(batch, wide * grp - lead)
        flip[:, 0 : many * depth] = jnp.transpose(src_ref[lead * depth : (lead + many) * depth, :])
        for near in range(many):
            for c in range(slots):
                slot = (lead + near) * slots + c

                @pl.when(list_ref[2 * group, slot] > 0)
                def _():
                    for k in range(6):
                        r, q = divmod(c * 6 + k, packs)
                        column = near * depth + r
                        spread[slot, k] = jnp.broadcast_to(
                            flip[q * stride : q * stride + stride, column : column + 1],
                            (stride, 128),
                        )

    for load in loads:
        load.wait()
    for copy in copies:
        copy.start()
    tiles = lanes // 128

    def one_target(t, carry):
        xs = [
            [aim[t, a, :, l * 128 : l * 128 + 128] for a in range(3)] for l in range(tiles)
        ]

        def step(p, sums):
            sums = list(sums)
            for half in range(2):
                s = list_ref[t, 2 * p + half]
                for j in range(0, stride, 8):
                    y = [spread[s, a, j : j + 8, :] for a in range(3)]
                    f = [spread[s, 3 + a, j : j + 8, :] for a in range(3)]
                    for l in range(tiles):
                        d = [xs[l][a] - y[a] for a in range(3)]
                        dist = (d[0] * d[0] + d[1] * d[1]) + d[2] * d[2] + soft_square
                        inv = lax.rsqrt(dist)
                        cube = inv * inv * inv
                        dot = d[0] * f[0] + d[1] * f[1] + d[2] * f[2]
                        near = (dist + soft_square) * cube
                        far = dot * cube
                        for a in range(3):
                            sums[l * 3 + a] = sums[l * 3 + a] + (f[a] * near + d[a] * far)
            return tuple(sums)

        zero = tuple(jnp.zeros((8, 128), jnp.float32) for _ in range(3 * tiles))
        sums = lax.fori_loop(0, (list_ref[group + t, 0] + 1) // 2, step, zero)
        for l in range(tiles):
            for a in range(3):
                heap[t, a, :, l * 128 : l * 128 + 128] = sums[l * 3 + a]
        return carry

    lax.fori_loop(0, group, one_target, 0)
    for t in range(group):
        for a in range(3):
            row = (a * slots + t % slots) * tiles
            whole = jnp.sum(heap[t, a], axis=0, keepdims=True)
            for l in range(tiles):
                acc[t // slots, row + l : row + l + 1, :] = whole[:, l * 128 : l * 128 + 128]
    acc_ref[...] = acc[...].astype(acc_ref.dtype)
    for copy in copies:
        copy.wait()


def scatter_kernel(slots, grp, part_ref, self_ref, live_ref, vel_ref, got, send, recv):
    n = self_ref.shape[2]
    tiles = part_ref.shape[1] // (3 * slots)
    me = lax.axis_index("grp")
    barrier = pltpu.get_barrier_semaphore()
    for off in range(1, grp):
        pl.semaphore_signal(
            barrier, inc=1, device_id={"grp": lax.rem(me + off, grp)}, device_id_type=MESH
        )
    pl.semaphore_wait(barrier, grp - 1)
    copies = []
    for off in range(1, grp):
        peer = lax.rem(me + off, grp)
        copies.append(
            pltpu.make_async_remote_copy(
                src_ref=part_ref.at[peer],
                dst_ref=got.at[off],
                send_sem=send.at[off],
                recv_sem=recv.at[off],
                device_id={"grp": peer},
                device_id_type=MESH,
            )
        )
    for copy in copies:
        copy.start()
    total = part_ref[me].astype(jnp.float32)
    for index, copy in enumerate(copies):
        copy.wait()
        total = total + got[index + 1].astype(jnp.float32)
    for a in range(3):
        for c in range(slots):
            row = (a * slots + c) * tiles
            line = jnp.concatenate([total[row + l : row + l + 1] for l in range(tiles)], axis=1)
            value = self_ref[a, c : c + 1, :] + line[:, :n]
            vel_ref[a, c : c + 1, :] = value * live_ref[c].astype(jnp.float32)


def on_device(shapes, density, quad_weight, live, neighbor, rotation):
    slots, _, n = shapes.shape
    caps = neighbor.shape[1]
    grp = lax.axis_size("grp")
    wide = lax.axis_size("wide")
    group = grp * slots
    rows = up(4 * slots, 8)
    lanes = up(max(n, caps), 128)
    width = up(caps, 128)
    tall = up(n, 16)
    chunk = -(-n // grp)
    stride = up(chunk, 8)
    span = 128
    packs = (span - slots) // stride
    depth = -(-6 * slots // packs)
    flat_shapes = shapes.transpose(1, 0, 2)
    flat_density = density.transpose(1, 0, 2)
    vmem = pl.BlockSpec(memory_space=pltpu.VMEM)
    smem = pl.BlockSpec(memory_space=pltpu.SMEM)
    any_space = pl.BlockSpec(memory_space=pl.ANY)
    ops6, self_velocity, targets, sources, lists = pl.pallas_call(
        functools.partial(gather_kernel, slots, grp, wide, rows, chunk, stride, packs),
        out_shape=(
            jax.ShapeDtypeStruct((slots, 6, n, n), jnp.bfloat16),
            jax.ShapeDtypeStruct((3, slots, n), jnp.float32),
            jax.ShapeDtypeStruct((grp, rows, lanes), jnp.float32),
            jax.ShapeDtypeStruct((wide * grp * depth, span), jnp.float32),
            jax.ShapeDtypeStruct((2 * group + 8, width), jnp.int32),
        ),
        in_specs=[vmem, vmem, vmem, smem, vmem, vmem],
        out_specs=(any_space,) + (vmem,) * 4,
        scratch_shapes=[
            pltpu.VMEM((slots, 6, n, n), jnp.bfloat16),
            pltpu.SemaphoreType.DMA((slots,)),
            pltpu.VMEM((rows, lanes), jnp.float32),
            pltpu.VMEM((slots, 8, lanes), jnp.float32),
            pltpu.VMEM((grp, depth, span), jnp.float32),
            pltpu.VMEM((grp, rows, lanes), jnp.float32),
            pltpu.VMEM((wide * grp, depth, span), jnp.float32),
            pltpu.VMEM((6, tall, n), jnp.bfloat16),
            pltpu.VMEM((lanes, 8), jnp.float32),
            pltpu.VMEM((n, lanes + 8), jnp.bfloat16),
            pltpu.VMEM((lanes, 8), jnp.float32),
            pltpu.SemaphoreType.DMA((grp,)),
            pltpu.SemaphoreType.DMA((grp,)),
            pltpu.SemaphoreType.DMA((wide * grp,)),
            pltpu.SemaphoreType.DMA((wide * grp,)),
        ],
        compiler_params=pltpu.CompilerParams(collective_id=0, has_side_effects=True),
        name="gather_ops",
    )(flat_shapes, flat_density, quad_weight, live, neighbor, rotation)
    blocks, partial = pl.pallas_call(
        functools.partial(pair_kernel, slots, grp, wide, rows, stride, packs),
        out_shape=(
            jax.ShapeDtypeStruct((slots, 3, 3, n, n), jnp.bfloat16),
            jax.ShapeDtypeStruct((grp, 3 * slots * lanes // 128, 128), jnp.bfloat16),
        ),
        in_specs=[smem, any_space, vmem, vmem],
        out_specs=(any_space, vmem),
        scratch_shapes=[
            pltpu.VMEM((grp, 3 * slots * lanes // 128, 128), jnp.float32),
            pltpu.VMEM((slots, 6, n, n), jnp.bfloat16),
            pltpu.SemaphoreType.DMA((slots,)),
            pltpu.VMEM((caps + 1, 6, stride, 128), jnp.float32),
            pltpu.VMEM((span, 128), jnp.float32),
            pltpu.VMEM((group, 3, 8, lanes), jnp.float32),
            pltpu.VMEM((group, 3, 8, lanes), jnp.float32),
            pltpu.SemaphoreType.DMA((9 * slots,)),
        ],
        name="pair_sums",
    )(lists, ops6, targets, sources)
    velocity = pl.pallas_call(
        functools.partial(scatter_kernel, slots, grp),
        out_shape=jax.ShapeDtypeStruct((3, slots, n), jnp.float32),
        in_specs=[vmem, vmem, smem],
        out_specs=vmem,
        scratch_shapes=[
            pltpu.VMEM((grp, 3 * slots * lanes // 128, 128), jnp.bfloat16),
            pltpu.SemaphoreType.DMA((grp,)),
            pltpu.SemaphoreType.DMA((grp,)),
        ],
        compiler_params=pltpu.CompilerParams(collective_id=1, has_side_effects=True),
        name="scatter_sums",
    )(partial, self_velocity, live)
    return (blocks.transpose(0, 1, 3, 2, 4), velocity.transpose(1, 0, 2))


def solution(mesh):
    placed = (
        P(("wide", "grp"), None, None),
        P(("wide", "grp"), None, None),
        P(("wide", "grp"), None),
        P(("wide", "grp")),
        P(("wide", "grp"), None),
        P(),
    )
    return jax.shard_map(
        on_device,
        mesh=mesh,
        in_specs=placed,
        out_specs=(P(("wide", "grp"), None, None, None, None), P(("wide", "grp"), None, None)),
        check_vma=False,
    )
```

```python
import functools
import jax
import jax.numpy as jnp
from jax import lax
from jax.experimental import pallas as pl
from jax.experimental.pallas import tpu as pltpu
from jax.sharding import PartitionSpec as P

soft_square = 0.0625
MESH = pl.DeviceIdType.MESH
SYM = ((0, 0), (0, 1), (0, 2), (1, 1), (1, 2), (2, 2))


def up(value, step):
    return (value + step - 1) // step * step


def split3(x):
    hi = x.astype(jnp.bfloat16)
    rest = x - hi.astype(jnp.float32)
    mid = rest.astype(jnp.bfloat16)
    low = (rest - mid.astype(jnp.float32)).astype(jnp.bfloat16)
    return hi, mid, low


def gather_kernel(
    slots, grp, wide, rows, chunk, stride, packs,
    shape_ref, dens_ref, qw_ref, live_ref, nbr_ref, rot_ref,
    ops_ref, vel_ref, tgt_ref, src_ref, list_ref,
    ops_buf, ops_sem, own, mats, parts, gbuf, cbuf, kern, cols, table, sums, gsend, grecv, csend, crecv,
):
    n = rot_ref.shape[0]
    lanes = own.shape[1]
    span = parts.shape[2]
    caps = nbr_ref.shape[1]
    me_g = lax.axis_index("grp")
    me_w = lax.axis_index("wide")
    me = me_w * grp + me_g
    barrier = pltpu.get_barrier_semaphore()
    peers = [(dw, dg) for dw in range(wide) for dg in range(grp) if dw or dg]

    def place(dw, dg):
        return {"wide": lax.rem(me_w + dw, wide), "grp": lax.rem(me_g + dg, grp)}

    for dw, dg in peers:
        pl.semaphore_signal(barrier, inc=1, device_id=place(dw, dg), device_id_type=MESH)

    own[...] = jnp.zeros_like(own)
    mats[...] = jnp.zeros_like(mats)
    alive = [live_ref[c].astype(jnp.float32) for c in range(slots)]
    for c in range(slots):
        for a in range(3):
            row = shape_ref[a, c : c + 1, :]
            own[a * slots + c : a * slots + c + 1, 0:n] = row
            mats[c, a : a + 1, 0:n] = row
            mats[c, 3 + a : 4 + a, 0:n] = qw_ref[c : c + 1, :] * dens_ref[a, c : c + 1, :] * alive[c]
        own[3 * slots + c : 3 * slots + c + 1, 0:caps] = (
            nbr_ref[c : c + 1, :].astype(jnp.float32) * alive[c]
        )
    lane = lax.broadcasted_iota(jnp.int32, (1, span), 1)
    tag = jnp.zeros((1, span), jnp.float32)
    for c in range(slots):
        tag = jnp.where(lane == packs * stride + c, alive[c], tag)
    for g in range(grp):
        for r in range(parts.shape[1]):
            made = tag
            for q in range(packs):
                c, k = divmod(r * packs + q, 6)
                if c < slots:
                    moved = pltpu.roll(mats[c], (q * stride - g * chunk) % lanes, axis=1)
                    inside = (lane >= q * stride) & (lane < q * stride + chunk)
                    made = jnp.where(inside, moved[k : k + 1, 0:span], made)
            parts[g, r : r + 1, :] = made

    pl.semaphore_wait(barrier, len(peers))
    copies = []
    for dw, dg in peers:
        copies.append(
            pltpu.make_async_remote_copy(
                src_ref=parts.at[lax.rem(me_g + dg, grp)],
                dst_ref=cbuf.at[me],
                send_sem=csend.at[dw * grp + dg],
                recv_sem=crecv.at[dw * grp + dg],
                device_id=place(dw, dg),
                device_id_type=MESH,
            )
        )
    for dg in range(1, grp):
        copies.append(
            pltpu.make_async_remote_copy(
                src_ref=own,
                dst_ref=gbuf.at[me_g],
                send_sem=gsend.at[dg],
                recv_sem=grecv.at[dg],
                device_id=place(0, dg),
                device_id_type=MESH,
            )
        )
    for copy in copies:
        copy.start()

    rot = rot_ref[...]
    table[...] = jnp.zeros_like(table)
    table[:, 0:n] = rot
    few = lax.broadcasted_iota(jnp.int32, (n, 8), 1)
    tall = lax.broadcasted_iota(jnp.int32, (kern.shape[1], 8), 1)
    for c in range(slots):
        pos = jnp.concatenate([shape_ref[a, c : c + 1, :] for a in range(3)], axis=0)
        nodes = None
        for piece in split3(pos):
            part = lax.dot_general(
                piece, rot, (((1,), (1,)), ((), ())), preferred_element_type=jnp.float32
            )
            nodes = part if nodes is None else nodes + part
        weight = qw_ref[c : c + 1, :]
        cols[...] = jnp.transpose(mats[c])
        force = [dens_ref[b, c : c + 1, :] for b in range(3)]
        force = jnp.concatenate(force + force + [jnp.zeros((2, n), jnp.float32)], axis=0)
        force = jnp.concatenate([force, jnp.zeros((8, lanes - n), jnp.float32)], axis=1)
        turned = jnp.transpose(force)[0:n].astype(jnp.bfloat16)
        pushed = jnp.dot(rot, turned, preferred_element_type=jnp.float32)
        coarse = pushed.astype(jnp.bfloat16).astype(jnp.float32)
        table[:, lanes : lanes + 8] = jnp.where(few < 3, coarse, pushed - coarse).astype(jnp.bfloat16)

        def block_step(step, carry):
            start = pl.multiple_of(step * 16, 16)
            block = cols[pl.ds(start, 16), :]
            diff = [block[:, a : a + 1] - nodes[a : a + 1, :] for a in range(3)]
            dist = diff[0] * diff[0] + diff[1] * diff[1] + diff[2] * diff[2]
            inv = lax.rsqrt(dist + soft_square)
            scaled = inv * inv * inv * weight
            half = [d * scaled for d in diff]
            diag = (dist + 2.0 * soft_square) * scaled
            for index, (a, b) in enumerate(SYM):
                value = half[a] * diff[b]
                if a == b:
                    value = value + diag
                kern[index, pl.ds(start, 16), :] = value.astype(jnp.bfloat16)
            return carry

        steps = kern.shape[1] // 16
        lax.fori_loop(0, steps, block_step, 0, unroll=4 if steps % 4 == 0 else 1)
        total = [jnp.zeros((kern.shape[1], 8), jnp.float32) for _ in range(3)]
        for index, (a, b) in enumerate(SYM):
            product = jnp.dot(kern[index], table[...], preferred_element_type=jnp.float32)
            ops_buf[c, index] = jnp.where(alive[c] > 0.0, product[:n, :n], 0.0).astype(jnp.bfloat16)
            column = product[:, lanes : lanes + 8]
            total[a] = total[a] + jnp.where((tall == b) | (tall == 3 + b), column, 0.0)
            if a != b:
                total[b] = total[b] + jnp.where((tall == a) | (tall == 3 + a), column, 0.0)
        for a in range(3):
            sums[...] = jnp.zeros_like(sums)
            sums[0 : kern.shape[1], :] = total[a]
            row = jnp.sum(jnp.transpose(sums[...]), axis=0, keepdims=True)
            vel_ref[a, c : c + 1, :] = row[:, :n]
        store = pltpu.make_async_copy(ops_buf.at[c], ops_ref.at[c], ops_sem.at[c])
        store.start()
        copies.append(store)

    gbuf[me_g] = own[...]
    cbuf[me] = parts[me_g]
    for copy in copies:
        copy.wait()
    tgt_ref[...] = gbuf[...]
    depth = cbuf.shape[1]
    for d in range(wide * grp):
        src_ref[d * depth : d * depth + depth, :] = cbuf[d]
    group = grp * slots
    width = list_ref.shape[1]
    first = jnp.concatenate([cbuf[d, 0:1, :] for d in range(wide * grp)], axis=0)
    source_row = lax.broadcasted_iota(jnp.int32, (wide * grp, width), 0)
    source_col = lax.broadcasted_iota(jnp.int32, (wide * grp, width), 1)
    living = jnp.zeros((1, width), jnp.float32)
    for c in range(slots):
        flag = first[:, packs * stride + c : packs * stride + c + 1]
        living = living + jnp.sum(
            jnp.where(source_col == source_row * slots + c, flag, 0.0), axis=0, keepdims=True
        )
    wanted = jnp.concatenate(
        [gbuf[g, 3 * slots : 4 * slots, 0:width] for g in range(grp)], axis=0
    )
    slot_row = lax.broadcasted_iota(jnp.int32, (group, width), 0) + me_w * group
    slot_col = lax.broadcasted_iota(jnp.int32, (group, width), 1)
    wanted = jnp.where((wanted * living > 0.0) & (slot_row != slot_col), 1.0, 0.0)
    before = lax.broadcasted_iota(jnp.int32, (width, width), 0)
    after = lax.broadcasted_iota(jnp.int32, (width, width), 1)
    lower = jnp.where(before < after, 1.0, 0.0).astype(jnp.bfloat16)
    rank = jnp.dot(wanted.astype(jnp.bfloat16), lower, preferred_element_type=jnp.float32)
    rank = jnp.where(wanted > 0.0, rank, -1.0)
    rank_cols = jnp.transpose(rank)
    seat = lax.broadcasted_iota(jnp.int32, (caps, width), 1).astype(jnp.float32)
    name = (lax.broadcasted_iota(jnp.int32, (caps, width), 0) - caps).astype(jnp.float32)
    for t in range(group):
        here = jnp.where(rank_cols[0:caps, t : t + 1] == seat, name, 0.0)
        ids = jnp.sum(here, axis=0, keepdims=True) + caps
        list_ref[t : t + 1, :] = ids.astype(jnp.int32)
    counts = jnp.sum(wanted, axis=1, keepdims=True)
    list_ref[group : 2 * group, :] = jnp.broadcast_to(counts, (group, width)).astype(jnp.int32)
    list_ref[2 * group : 2 * group + 8, :] = jnp.broadcast_to(living, (8, width)).astype(jnp.int32)


def pair_kernel(
    slots, grp, wide, rows, stride, packs,
    list_ref, ops_ref, tgt_ref, src_ref,
    out_ref, acc_ref, ops_buf, ops_sem, spread, flip, aim, heap, sems,
):
    lanes = tgt_ref.shape[2]
    group = grp * slots
    caps = wide * group
    loads = [
        pltpu.make_async_copy(ops_ref.at[c], ops_buf.at[c], ops_sem.at[c]) for c in range(slots)
    ]
    for load in loads:
        load.start()
    copies = []
    for c in range(slots):
        for a in range(3):
            for b in range(3):
                index = SYM.index((min(a, b), max(a, b)))
                copies.append(
                    pltpu.make_async_copy(
                        ops_buf.at[c, index], out_ref.at[c, a, b], sems.at[len(copies)]
                    )
                )
    for t in range(group):
        for a in range(3):
            row = a * slots + t % slots
            aim[t, a] = jnp.broadcast_to(tgt_ref[t // slots, row : row + 1, :], (8, lanes))
    spread[caps] = jnp.zeros_like(spread[caps])
    depth = src_ref.shape[0] // (wide * grp)
    batch = 128 // up(depth, 4)
    for lead in range(0, wide * grp, batch):
        many = min(batch, wide * grp - lead)
        flip[:, 0 : many * depth] = jnp.transpose(src_ref[lead * depth : (lead + many) * depth, :])
        for near in range(many):
            for c in range(slots):
                slot = (lead + near) * slots + c

                @pl.when(list_ref[2 * group, slot] > 0)
                def _():
                    for k in range(6):
                        r, q = divmod(c * 6 + k, packs)
                        column = near * depth + r
                        spread[slot, k] = jnp.broadcast_to(
                            flip[q * stride : q * stride + stride, column : column + 1],
                            (stride, 128),
                        )

    for load in loads:
        load.wait()
    for copy in copies:
        copy.start()
    tiles = lanes // 128

    def one_target(t, carry):
        xs = [
            [aim[t, a, :, l * 128 : l * 128 + 128] for a in range(3)] for l in range(tiles)
        ]

        def step(p, sums):
            sums = list(sums)
            for half in range(2):
                s = list_ref[t, 2 * p + half]
                for j in range(0, stride, 8):
                    y = [spread[s, a, j : j + 8, :] for a in range(3)]
                    f = [spread[s, 3 + a, j : j + 8, :] for a in range(3)]
                    for l in range(tiles):
                        d = [xs[l][a] - y[a] for a in range(3)]
                        dist = (d[0] * d[0] + d[1] * d[1]) + d[2] * d[2] + soft_square
                        inv = lax.rsqrt(dist)
                        cube = inv * inv * inv
                        dot = d[0] * f[0] + d[1] * f[1] + d[2] * f[2]
                        near = (dist + soft_square) * cube
                        far = dot * cube
                        for a in range(3):
                            sums[l * 3 + a] = sums[l * 3 + a] + (f[a] * near + d[a] * far)
            return tuple(sums)

        zero = tuple(jnp.zeros((8, 128), jnp.float32) for _ in range(3 * tiles))
        sums = lax.fori_loop(0, (list_ref[group + t, 0] + 1) // 2, step, zero)
        for l in range(tiles):
            for a in range(3):
                heap[t, a, :, l * 128 : l * 128 + 128] = sums[l * 3 + a]
        return carry

    lax.fori_loop(0, group, one_target, 0)
    for t in range(group):
        for a in range(3):
            row = (a * slots + t % slots) * tiles
            whole = jnp.sum(heap[t, a], axis=0, keepdims=True)
            for l in range(tiles):
                acc_ref[t // slots, row + l : row + l + 1, :] = whole[:, l * 128 : l * 128 + 128]
    for copy in copies:
        copy.wait()


def scatter_kernel(slots, grp, part_ref, self_ref, live_ref, vel_ref, got, send, recv):
    n = self_ref.shape[2]
    tiles = part_ref.shape[1] // (3 * slots)
    me = lax.axis_index("grp")
    barrier = pltpu.get_barrier_semaphore()
    for off in range(1, grp):
        pl.semaphore_signal(
            barrier, inc=1, device_id={"grp": lax.rem(me + off, grp)}, device_id_type=MESH
        )
    pl.semaphore_wait(barrier, grp - 1)
    copies = []
    for off in range(1, grp):
        peer = lax.rem(me + off, grp)
        copies.append(
            pltpu.make_async_remote_copy(
                src_ref=part_ref.at[peer],
                dst_ref=got.at[off],
                send_sem=send.at[off],
                recv_sem=recv.at[off],
                device_id={"grp": peer},
                device_id_type=MESH,
            )
        )
    for copy in copies:
        copy.start()
    total = part_ref[me]
    for index, copy in enumerate(copies):
        copy.wait()
        total = total + got[index + 1]
    for a in range(3):
        for c in range(slots):
            row = (a * slots + c) * tiles
            line = jnp.concatenate([total[row + l : row + l + 1] for l in range(tiles)], axis=1)
            value = self_ref[a, c : c + 1, :] + line[:, :n]
            vel_ref[a, c : c + 1, :] = value * live_ref[c].astype(jnp.float32)


def on_device(shapes, density, quad_weight, live, neighbor, rotation):
    slots, _, n = shapes.shape
    caps = neighbor.shape[1]
    grp = lax.axis_size("grp")
    wide = lax.axis_size("wide")
    group = grp * slots
    rows = up(4 * slots, 8)
    lanes = up(max(n, caps), 128)
    width = up(caps, 128)
    tall = up(n, 16)
    chunk = -(-n // grp)
    stride = up(chunk, 8)
    span = 128
    packs = (span - slots) // stride
    depth = -(-6 * slots // packs)
    flat_shapes = shapes.transpose(1, 0, 2)
    flat_density = density.transpose(1, 0, 2)
    vmem = pl.BlockSpec(memory_space=pltpu.VMEM)
    smem = pl.BlockSpec(memory_space=pltpu.SMEM)
    any_space = pl.BlockSpec(memory_space=pl.ANY)
    ops6, self_velocity, targets, sources, lists = pl.pallas_call(
        functools.partial(gather_kernel, slots, grp, wide, rows, chunk, stride, packs),
        out_shape=(
            jax.ShapeDtypeStruct((slots, 6, n, n), jnp.bfloat16),
            jax.ShapeDtypeStruct((3, slots, n), jnp.float32),
            jax.ShapeDtypeStruct((grp, rows, lanes), jnp.float32),
            jax.ShapeDtypeStruct((wide * grp * depth, span), jnp.float32),
            jax.ShapeDtypeStruct((2 * group + 8, width), jnp.int32),
        ),
        in_specs=[vmem, vmem, vmem, smem, vmem, vmem],
        out_specs=(any_space,) + (vmem,) * 4,
        scratch_shapes=[
            pltpu.VMEM((slots, 6, n, n), jnp.bfloat16),
            pltpu.SemaphoreType.DMA((slots,)),
            pltpu.VMEM((rows, lanes), jnp.float32),
            pltpu.VMEM((slots, 8, lanes), jnp.float32),
            pltpu.VMEM((grp, depth, span), jnp.float32),
            pltpu.VMEM((grp, rows, lanes), jnp.float32),
            pltpu.VMEM((wide * grp, depth, span), jnp.float32),
            pltpu.VMEM((6, tall, n), jnp.bfloat16),
            pltpu.VMEM((lanes, 8), jnp.float32),
            pltpu.VMEM((n, lanes + 8), jnp.bfloat16),
            pltpu.VMEM((lanes, 8), jnp.float32),
            pltpu.SemaphoreType.DMA((grp,)),
            pltpu.SemaphoreType.DMA((grp,)),
            pltpu.SemaphoreType.DMA((wide * grp,)),
            pltpu.SemaphoreType.DMA((wide * grp,)),
        ],
        compiler_params=pltpu.CompilerParams(collective_id=0, has_side_effects=True),
        name="gather_ops",
    )(flat_shapes, flat_density, quad_weight, live, neighbor, rotation)
    blocks, partial = pl.pallas_call(
        functools.partial(pair_kernel, slots, grp, wide, rows, stride, packs),
        out_shape=(
            jax.ShapeDtypeStruct((slots, 3, 3, n, n), jnp.bfloat16),
            jax.ShapeDtypeStruct((grp, 3 * slots * lanes // 128, 128), jnp.float32),
        ),
        in_specs=[smem, any_space, vmem, vmem],
        out_specs=(any_space, vmem),
        scratch_shapes=[
            pltpu.VMEM((slots, 6, n, n), jnp.bfloat16),
            pltpu.SemaphoreType.DMA((slots,)),
            pltpu.VMEM((caps + 1, 6, stride, 128), jnp.float32),
            pltpu.VMEM((span, 128), jnp.float32),
            pltpu.VMEM((group, 3, 8, lanes), jnp.float32),
            pltpu.VMEM((group, 3, 8, lanes), jnp.float32),
            pltpu.SemaphoreType.DMA((9 * slots,)),
        ],
        name="pair_sums",
    )(lists, ops6, targets, sources)
    velocity = pl.pallas_call(
        functools.partial(scatter_kernel, slots, grp),
        out_shape=jax.ShapeDtypeStruct((3, slots, n), jnp.float32),
        in_specs=[vmem, vmem, smem],
        out_specs=vmem,
        scratch_shapes=[
            pltpu.VMEM((grp, 3 * slots * lanes // 128, 128), jnp.float32),
            pltpu.SemaphoreType.DMA((grp,)),
            pltpu.SemaphoreType.DMA((grp,)),
        ],
        compiler_params=pltpu.CompilerParams(collective_id=1, has_side_effects=True),
        name="scatter_sums",
    )(partial, self_velocity, live)
    return (blocks.transpose(0, 1, 3, 2, 4), velocity.transpose(1, 0, 2))


def solution(mesh):
    placed = (
        P(("wide", "grp"), None, None),
        P(("wide", "grp"), None, None),
        P(("wide", "grp"), None),
        P(("wide", "grp")),
        P(("wide", "grp"), None),
        P(),
    )
    return jax.shard_map(
        on_device,
        mesh=mesh,
        in_specs=placed,
        out_specs=(P(("wide", "grp"), None, None, None, None), P(("wide", "grp"), None, None)),
        check_vma=False,
    )
```
